32 devices in a mesh: section: 2 (over y), tensor: 4 (over x, core), dp: 4 (over z).
Axes of the slice: x: 2, y: 2, z: 4, core: 2. Of those that a mesh axis runs over, the one named last changes fastest.
Arguments:
- hidden: bfloat16 [2, 8, 256, 14336], P('section', 'dp', None, 'tensor'), parts along dimension 1, may hold values from -6 to 6
- down_weight: bfloat16 [2, 14336, 4096], P('section', 'tensor'), may hold values from -0.046875 to 0.046875
- residual: bfloat16 [2, 8, 256, 4096], P('section', 'dp', 'tensor'), parts along dimension 1, may hold values from -6 to 6
- norm_gain: float32 [2, 4096], P('section'), may hold values from 0.1 to 1.9
- qkv_weight: bfloat16 [2, 4096, 5120], P('section', None, 'tensor'), may hold values from -0.09375 to 0.09375
Outputs:
- carried: bfloat16 [2, 8, 256, 4096], P('section', 'dp', 'tensor'), parts along dimension 1
- attention_inputs: bfloat16 [2, 8, 256, 5120], P('section', 'dp', None, 'tensor'), parts along dimension 1
The draws below stay inside these ranges and needn't reach their ends.
There are 4 independent parts, one for each index of `dp`. The reference program is written for one: setup_inputs(seed, part) draws one part's arguments, and reference() takes and returns one part's arrays. A program takes and returns all parts, laid end to end along the dimension named above; an argument that names none is the same for every part. Nothing has to cross between parts.
All inputs are finite; a program needn't handle non-finite values.
Results may differ from the reference program's by a relative error of at most 0.012.
Values may be sent and summed in bfloat16 or wider, within the bound.
A program may use at most 128 MiB of HBM per device.

```python
import jax
import jax.numpy as jnp
from jax import lax

D = 4096
FF = 14336
QKV = 5120
MB = 2
TOK = 256
SECTIONS = 2
N_TENSOR = 4


def level_of(own_key, extent, pieces, smallest, largest):
    loudness, own = 1.0, jax.random.fold_in(own_key, 6)
    for position, parts in pieces:
        heights = jnp.exp(jax.random.uniform(jax.random.fold_in(own, position), (parts,), jnp.float32, smallest / len(pieces), largest / len(pieces)))
        loudness = loudness * jnp.repeat(heights, extent[position] // parts).reshape([-1 if axis == position else 1 for axis in range(len(extent))])
    return loudness


def scatter_about(key, shape, deviation, reach, cuts=(), held_as=jnp.bfloat16):
    values = deviation * jax.random.normal(key, shape, jnp.float32)
    if cuts:
        values = values * level_of(key, shape, cuts, -0.22, 0.18)
    return jnp.clip(values, -reach, reach).astype(held_as)


def setup_inputs(seed: int = 0, part: int = 0) -> dict:
    splits = jax.random.split(jax.random.key(seed), 6)
    part_splits = jax.random.split(jax.random.fold_in(splits[5], part), 6)
    hidden = scatter_about(part_splits[0], (SECTIONS, MB, TOK, FF), 1.0, 6.0, ((0, 2), (3, 4)))
    down_weight = scatter_about(splits[1], (SECTIONS, FF, D), FF ** -0.5, 0.046875, ((0, 2), (1, 4)))
    residual = scatter_about(part_splits[2], (SECTIONS, MB, TOK, D), 1.0, 6.0, ((0, 2), (2, 4)))
    norm_gain = jnp.clip(1.0 + 0.18 * jax.random.normal(splits[3], (SECTIONS, D), jnp.float32), 0.1, 1.9)
    qkv_weight = scatter_about(splits[4], (SECTIONS, D, QKV), D ** -0.5, 0.09375, ((0, 2), (2, 4)))
    return {"hidden": hidden, "down_weight": down_weight, "residual": residual, "norm_gain": norm_gain, "qkv_weight": qkv_weight}


def section_stream(hidden_s, weight_s, residual_s):
    block = FF // N_TENSOR
    rows = hidden_s.reshape(MB * TOK, FF)

    def add_block(total, block_index):
        first = (block_index * block).astype(jnp.int32)
        hidden_part = lax.dynamic_slice_in_dim(rows, first, block, 1)
        weight_part = lax.dynamic_slice_in_dim(weight_s, first, block, 0)
        partial_value = jnp.dot(hidden_part, weight_part, preferred_element_type=jnp.float32).astype(jnp.bfloat16)
        partial_value = lax.optimization_barrier(partial_value)
        return (total + partial_value.astype(jnp.float32), None)
    start_total = jnp.zeros((MB * TOK, D), jnp.float32)
    total, _ = lax.scan(add_block, start_total, jnp.arange(N_TENSOR, dtype=jnp.int32))
    summed = total.reshape(MB, TOK, D) + residual_s.astype(jnp.float32)
    return summed.astype(jnp.bfloat16)

def reference(hidden, down_weight, residual, norm_gain, qkv_weight):
    streams = jnp.stack([section_stream(hidden[s], down_weight[s], residual[s]) for s in range(SECTIONS)])
    carried = jnp.roll(streams, 1, axis=0)
    outputs = []
    for s in range(SECTIONS):
        values = carried[s].astype(jnp.float32)
        mean_square = lax.optimization_barrier(jnp.mean(values * values, axis=-1, keepdims=True))
        normed = (values * lax.rsqrt(mean_square + 1e-05) * norm_gain[s][None, None, :]).astype(jnp.bfloat16)
        projected = jnp.dot(normed.reshape(MB * TOK, D), qkv_weight[s], preferred_element_type=jnp.float32)
        outputs.append(projected.astype(jnp.bfloat16).reshape(MB, TOK, QKV))
    return (carried, jnp.stack(outputs))
```

```python
import functools

import jax
import jax.numpy as jnp
from jax import lax
from jax.experimental import pallas as pl
from jax.experimental.pallas import tpu as pltpu
from jax.sharding import PartitionSpec as P

MESH = pl.DeviceIdType.MESH
F32 = jnp.float32
BF16 = jnp.bfloat16
CHUNKS = 8
SLABS = 3
LAG_SUM, LAG_HAND, LAG_PASS, LAG_PROJ = 2, 4, 5, 6


def kernel(
    sections, tensor, hidden, weight, residual, gain_in, projector,
    carried_out, projected_out,
    rows, slab, qkv, res, gain, own, held, core_send, core_recv, x_send, x_recv, base, stream, carried, acc, squares,
    hidden_sem, slab_sem, first_sem, qkv_sem, res_sem, gain_sem, carried_sem,
    core_ss, core_rs, half_ss, half_rs, x_ss, x_rs, y_ss, y_rs, g_ss, g_rs, c_ss, c_rs,
):
    chips = tensor // 2
    chunks, _, micro, local, piece = stream.shape
    width = 2 * piece
    features = chunks * width
    depth = rows.shape[-1]
    cut = pl.cdiv(depth // 2, 128) * 128
    lines = chips * micro * local
    last = chunks - 1
    s = lax.axis_index("section")
    t = lax.axis_index("tensor")
    chip, core = t // 2, lax.rem(t, 2)
    sibling = chip * 2 + 1 - core
    following = lax.rem(s + 1, sections)
    previous = lax.rem(s + sections - 1, sections)

    def ahead(j):
        return lax.rem(chip + j, chips)

    def behind(j):
        return lax.rem(chip + chips - j, chips)

    def deep(part):
        return slice(0, cut) if part == 0 else slice(cut, depth)

    def columns(k):
        return pl.ds(pl.multiple_of(k * width, width), width)

    def hidden_copy(j, part, m, d):
        lane = 1 - core if part == 0 else core
        first = pl.multiple_of((ahead(j) * 2 + lane) * local, local)
        return pltpu.make_async_copy(
            hidden.at[0, m, pl.ds(first, local), deep(d)], rows.at[j, part, m, :, deep(d)], hidden_sem.at[j, part, m, d]
        )

    def hidden_all(j, d, act):
        for part in range(2):
            for m in range(micro):
                act(hidden_copy(j, part, m, d))

    def slab_copy(k, d):
        slot = lax.rem(k, SLABS)
        return pltpu.make_async_copy(
            weight.at[0, deep(d), columns(k)], slab.at[slot, deep(d)], slab_sem.at[slot, d]
        )

    def first_copy(h, d):
        across = slice(h * piece, (h + 1) * piece)
        return pltpu.make_async_copy(
            weight.at[0, deep(d), across], slab.at[0, deep(d), across], first_sem.at[h, d]
        )

    def qkv_copy(k):
        return pltpu.make_async_copy(projector.at[0, columns(k), :], qkv.at[k], qkv_sem.at[k])

    res_copy = pltpu.make_async_copy(residual.at[0], res, res_sem)
    gain_copy = pltpu.make_async_copy(gain_in, gain, gain_sem)

    def carried_copy(k, h):
        across = pl.ds(pl.multiple_of(k * width + h * piece, piece), piece)
        return pltpu.make_async_copy(
            carried.at[k, h, core, chip], carried_out.at[0, :, :, across], carried_sem.at[k, h]
        )

    def core_copy(k, j):
        return pltpu.make_async_remote_copy(
            src_ref=core_send.at[k, j], dst_ref=core_recv.at[k, j], send_sem=core_ss.at[k, j], recv_sem=core_rs.at[k, j],
            device_id={"tensor": sibling}, device_id_type=MESH,
        )

    def core_half(h, j):
        return pltpu.make_async_remote_copy(
            src_ref=core_send.at[0, j, h], dst_ref=core_recv.at[0, j, h],
            send_sem=half_ss.at[h, j - 1], recv_sem=half_rs.at[h, j - 1],
            device_id={"tensor": sibling}, device_id_type=MESH,
        )

    def x_copy(k, j):
        return pltpu.make_async_remote_copy(
            src_ref=x_send.at[k, j - 1], dst_ref=x_recv.at[k, j - 1],
            send_sem=x_ss.at[k, j - 1], recv_sem=x_rs.at[k, j - 1],
            device_id={"tensor": ahead(j) * 2 + core}, device_id_type=MESH,
        )

    def x_half(h, j):
        return pltpu.make_async_remote_copy(
            src_ref=x_send.at[0, j - 1, h], dst_ref=x_recv.at[0, j - 1, h],
            send_sem=x_ss.at[0, j - 1], recv_sem=x_rs.at[0, j - 1],
            device_id={"tensor": ahead(j) * 2 + core}, device_id_type=MESH,
        )

    def y_copy(k):
        return pltpu.make_async_remote_copy(
            src_ref=stream.at[k], dst_ref=carried.at[k, :, core, chip], send_sem=y_ss.at[k], recv_sem=y_rs.at[k],
            device_id={"section": following}, device_id_type=MESH,
        )

    def gather_copy(k, h, j, block):
        place = carried.at[k, h, core, block]
        return pltpu.make_async_remote_copy(
            src_ref=place, dst_ref=place, send_sem=g_ss.at[k, h, j - 1], recv_sem=g_rs.at[k, h, j - 1],
            device_id={"tensor": ahead(j) * 2 + core}, device_id_type=MESH,
        )

    def pass_copy(k, h, j, lane, block):
        place = carried.at[k, h, lane, block]
        return pltpu.make_async_remote_copy(
            src_ref=place, dst_ref=place, send_sem=c_ss.at[k, h, j], recv_sem=c_rs.at[k, h, j],
            device_id={"tensor": sibling}, device_id_type=MESH,
        )

    others = range(1, chips)
    for d in range(2):
        for j in others:
            hidden_all(j, d, lambda copy: copy.start())
        first_copy(0, d).start()

    barrier = pltpu.get_barrier_semaphore()
    pl.semaphore_signal(barrier, inc=1, device_id={"tensor": sibling}, device_id_type=MESH)
    for j in others:
        pl.semaphore_signal(barrier, inc=1, device_id={"tensor": ahead(j) * 2 + core}, device_id_type=MESH)
    pl.semaphore_signal(barrier, inc=1, device_id={"section": following}, device_id_type=MESH)
    if sections > 2:
        pl.semaphore_signal(barrier, inc=1, device_id={"section": previous}, device_id_type=MESH)

    acc[...] = jnp.zeros_like(acc)
    squares[...] = jnp.zeros_like(squares)

    def multiply(j, d, right):
        left = rows[j, :, :, :, d].reshape(2 * micro * local, -1)
        return jnp.dot(left, right, preferred_element_type=F32).reshape(2, micro, local, -1)

    def first_half(h, d):
        return slab[0, deep(d), h * piece:(h + 1) * piece]

    def first_product(h):
        for j in others:
            value = own[j - 1, h] + multiply(j, deep(1), first_half(h, 1))
            core_send[0, j, h] = value[0].astype(BF16)
            own[j - 1, h] = value

    for j in others:
        hidden_all(j, 0, lambda copy: copy.wait())
    first_copy(0, 0).wait()
    for d in range(2):
        first_copy(1, d).start()
    for j in others:
        own[j - 1, 0] = multiply(j, deep(0), first_half(0, 0))
    for j in others:
        hidden_all(j, 1, lambda copy: copy.wait())
    first_copy(0, 1).wait()
    for d in range(2):
        slab_copy(1, d).start()
    for d in range(2):
        hidden_all(0, d, lambda copy: copy.start())
    first_product(0)
    pl.semaphore_wait(barrier, chips + (2 if sections > 2 else 1))
    for j in others:
        core_half(0, j).start()
    first_copy(1, 0).wait()
    for j in others:
        own[j - 1, 1] = multiply(j, deep(0), first_half(1, 0))
    first_copy(1, 1).wait()
    for k in range(2, SLABS):
        for d in range(2):
            slab_copy(k, d).start()
    first_product(1)
    for j in others:
        core_half(1, j).start()

    def first_send(h):
        for j in others:
            core_half(h, j).wait_recv()
            x_send[0, j - 1, h] = (own[j - 1, h, 1] + core_recv[0, j, h].astype(F32)).astype(BF16)
            x_half(h, j).start()

    first_send(0)
    res_copy.start()
    gain_copy.start()

    def halves(ref, value):
        for h in range(2):
            ref[h] = value[..., h * piece:(h + 1) * piece].astype(ref.dtype)

    def project(k, side, parts):
        lane = core if side == 0 else 1 - core
        values = [carried[k, h, lane].reshape(lines, piece).astype(F32) for h in parts]
        values = values[0] if len(values) == 1 else jnp.concatenate(values, axis=-1)
        squared = values * values
        part = squared[:, :128]
        for first in range(128, values.shape[1], 128):
            part = part + squared[:, first:first + 128]
        squares[side] += part
        first = parts[0] * piece
        across = pl.ds(pl.multiple_of(k * width + first, piece), values.shape[1])
        scaled = (values * gain[:, across]).astype(BF16)
        acc[side] += jnp.dot(scaled, qkv[k, first:first + values.shape[1]], preferred_element_type=F32)

    def finish(side):
        lane = core if side == 0 else 1 - core
        mean = jnp.sum(squares[side], axis=-1, keepdims=True) * (1.0 / features)
        value = (acc[side] * lax.rsqrt(mean + 1e-05)).astype(BF16).reshape(chips, micro, local, -1)
        for c in range(chips):
            first = pl.multiple_of((c * 2 + lane) * local, local)
            for m in range(micro):
                projected_out[0, m, pl.ds(first, local), :] = value[c, m]

    def step(i, _):
        @pl.when(i < chunks)
        def _():
            slot = lax.rem(i, SLABS)
            for d in range(2):
                slab_copy(i, d).wait()
            for j in others:
                value = multiply(j, slice(None), slab[slot])
                halves(core_send.at[i, j], value[0])
                core_copy(i, j).start()
                halves(held.at[j - 1], value[1])

        @pl.when(i == 1)
        def _():
            first_send(1)
            for d in range(2):
                hidden_all(0, d, lambda copy: copy.wait())

        @pl.when(i <= chunks)
        def _():
            k = i - 1
            value = multiply(0, slice(None), slab[lax.rem(k, SLABS)])
            halves(core_send.at[k, 0], value[0])
            core_copy(k, 0).start()
            halves(base.at[k], value[1])

            @pl.when(k + SLABS < chunks)
            def _():
                for d in range(2):
                    slab_copy(k + SLABS, d).start()

        @pl.when(i < chunks)
        def _():
            for j in others:
                core_copy(i, j).wait_recv()
                x_send[i, j - 1] = (held[j - 1] + core_recv[i, j].astype(F32)).astype(BF16)
                x_copy(i, j).start()

        k_sum = i - LAG_SUM

        @pl.when((k_sum >= 0) & (k_sum < chunks))
        def _():
            k = k_sum

            @pl.when(k == 0)
            def _():
                res_copy.wait()
                gain_copy.wait()

            qkv_copy(k).start()
            core_copy(k, 0).wait_recv()
            value = base[k] + core_recv[k, 0].astype(F32)
            for j in others:
                x_copy(k, j).wait_recv()
                value = value + x_recv[k, j - 1].astype(F32)
            added = res[:, :, columns(k)].astype(F32)
            for h in range(2):
                stream[k, h] = (value[h] + added[..., h * piece:(h + 1) * piece]).astype(BF16)
            y_copy(k).start()

        k_hand = i - LAG_HAND

        @pl.when((k_hand >= 0) & (k_hand < chunks))
        def _():
            k = k_hand
            y_copy(k).wait_recv()
            for h in range(2):
                for j in others:
                    gather_copy(k, h, j, chip).start()
                pass_copy(k, h, 0, core, chip).start()
            for h in range(2):
                carried_copy(k, h).start()

        k_proj = i - LAG_PROJ

        @pl.when((k_proj >= 0) & (k_proj < last))
        def _():
            k = k_proj
            for h in range(2):
                for j in range(chips):
                    pass_copy(k, h, j, 1 - core, behind(j)).wait_recv()
            project(k, 1, (0, 1))

        k_pass = i - LAG_PASS

        @pl.when((k_pass >= 0) & (k_pass < last))
        def _():
            k = k_pass
            for h in range(2):
                for j in others:
                    gather_copy(k, h, j, behind(j)).wait_recv()
                    pass_copy(k, h, j, core, behind(j)).start()
            qkv_copy(k).wait()
            project(k, 0, (0, 1))

        return 0

    lax.fori_loop(1, last + LAG_PROJ, step, 0)

    qkv_copy(last).wait()
    for h in range(2):
        for j in others:
            gather_copy(last, h, j, behind(j)).wait_recv()
            pass_copy(last, h, j, core, behind(j)).start()
        project(last, 0, (h,))
    finish(0)
    for h in range(2):
        for j in range(chips):
            pass_copy(last, h, j, 1 - core, behind(j)).wait_recv()
        project(last, 1, (h,))
    finish(1)

    for j in others:
        for h in range(2):
            core_half(h, j).wait_send()

    def drain(k, _):
        core_copy(k, 0).wait_send()
        y_copy(k).wait_send()
        for h in range(2):
            carried_copy(k, h).wait()
            pass_copy(k, h, 0, core, chip).wait_send()
        for j in others:
            @pl.when(k > 0)
            def _():
                core_copy(k, j).wait_send()

            x_copy(k, j).wait_send()
            for h in range(2):
                gather_copy(k, h, j, chip).wait_send()
                pass_copy(k, h, j, core, behind(j)).wait_send()
        return 0

    lax.fori_loop(0, chunks, drain, 0)


def leave(carried_in, projected_in, carried_out, projected_out, sems):
    copies = [
        pltpu.make_async_copy(carried_in, carried_out, sems.at[0]),
        pltpu.make_async_copy(projected_in, projected_out, sems.at[1]),
    ]
    for copy in copies:
        copy.start()
    for copy in copies:
        copy.wait()


def per_device(sections, tensor, hidden, down_weight, residual, norm_gain, qkv_weight):
    _, micro, tokens, depth = hidden.shape
    local, features = residual.shape[2:]
    outputs = qkv_weight.shape[2]
    chips = tensor // 2
    chunks = CHUNKS
    width = features // chunks
    piece = width // 2
    dma = pltpu.SemaphoreType.DMA
    anywhere = pl.BlockSpec(memory_space=pl.ANY)
    carried_shape = (1, micro, local, features)
    projected_shape = (1, micro, tokens, outputs)
    results = pl.pallas_call(
        functools.partial(kernel, sections, tensor),
        out_shape=(pltpu.VMEM(carried_shape, BF16), pltpu.VMEM(projected_shape, BF16)),
        in_specs=[pl.BlockSpec(memory_space=pltpu.HBM)] * 5,
        out_specs=(pl.BlockSpec(memory_space=pltpu.VMEM),) * 2,
        scratch_shapes=[
            pltpu.VMEM((chips, 2, micro, local, depth), BF16),
            pltpu.VMEM((SLABS, depth, width), BF16),
            pltpu.VMEM((chunks, width, outputs), BF16),
            pltpu.VMEM((micro, local, features), BF16),
            pltpu.VMEM((1, features), F32),
            pltpu.VMEM((chips - 1, 2, 2, micro, local, piece), F32),
            pltpu.VMEM((chips - 1, 2, micro, local, piece), F32),
            pltpu.VMEM((chunks, chips, 2, micro, local, piece), BF16),
            pltpu.VMEM((chunks, chips, 2, micro, local, piece), BF16),
            pltpu.VMEM((chunks, chips - 1, 2, micro, local, piece), BF16),
            pltpu.VMEM((chunks, chips - 1, 2, micro, local, piece), BF16),
            pltpu.VMEM((chunks, 2, micro, local, piece), F32),
            pltpu.VMEM((chunks, 2, micro, local, piece), BF16),
            pltpu.VMEM((chunks, 2, 2, chips, micro, local, piece), BF16),
            pltpu.VMEM((2, micro * tokens // 2, outputs), F32),
            pltpu.VMEM((2, micro * tokens // 2, 128), F32),
            dma((chips, 2, micro, 2)), dma((SLABS, 2)), dma((2, 2)), dma((chunks,)), dma, dma, dma((chunks, 2)),
            dma((chunks, chips)), dma((chunks, chips)), dma((2, chips - 1)), dma((2, chips - 1)),
            dma((chunks, chips - 1)), dma((chunks, chips - 1)),
            dma((chunks,)), dma((chunks,)),
            dma((chunks, 2, chips - 1)), dma((chunks, 2, chips - 1)),
            dma((chunks, 2, chips)), dma((chunks, 2, chips)),
        ],
        compiler_params=pltpu.CompilerParams(
            collective_id=0, has_side_effects=True, vmem_limit_bytes=52 * 1024 * 1024
        ),
    )(
        hidden,
        down_weight,
        pltpu.with_memory_space_constraint(residual, pltpu.HBM),
        pltpu.with_memory_space_constraint(norm_gain, pltpu.HBM),
        qkv_weight,
    )
    return pl.pallas_call(
        leave,
        out_shape=(
            jax.ShapeDtypeStruct(carried_shape, BF16),
            jax.ShapeDtypeStruct(projected_shape, BF16),
        ),
        in_specs=[anywhere] * 2,
        out_specs=(anywhere,) * 2,
        scratch_shapes=[dma((2,))],
    )(*(pltpu.with_memory_space_constraint(x, pltpu.VMEM) for x in results))


def solution(mesh):
    placed = (
        P("section", "dp", None, "tensor"),
        P("section", "tensor", None),
        P("section", "dp", "tensor", None),
        P("section", None),
        P("section", None, "tensor"),
    )
    return jax.shard_map(
        functools.partial(per_device, mesh.shape["section"], mesh.shape["tensor"]),
        mesh=mesh,
        in_specs=placed,
        out_specs=(P("section", "dp", "tensor", None), P("section", "dp", None, "tensor")),
        check_vma=False,
    )
```

```python
import functools

import jax
import jax.numpy as jnp
from jax import lax
from jax.experimental import pallas as pl
from jax.experimental.pallas import tpu as pltpu
from jax.sharding import PartitionSpec as P

MESH = pl.DeviceIdType.MESH
F32 = jnp.float32
BF16 = jnp.bfloat16
CHUNKS = 8
SLABS = 3
LAG_SUM, LAG_HAND = 3, 7


def kernel(
    sections, tensor, hidden, weight, residual, gain_in, projector,
    carried_out, projected_out,
    rows, slab, qkv, res, gain, own, held, core_send, core_recv, x_send, x_recv, base, stream, carried, acc, squares,
    hidden_sem, slab_sem, first_sem, qkv_sem, res_sem, gain_sem, carried_sem,
    core_ss, core_rs, half_ss, half_rs, mine_ss, mine_rs, x_ss, x_rs, y_ss, y_rs, g_ss, g_rs, c_ss, c_rs,
):
    chips = tensor // 2
    units, micro, local, piece = stream.shape
    chunks = units // 2
    width = 2 * piece
    features = units * piece
    depth = rows.shape[-1]
    cut = pl.cdiv(depth // 2, 128) * 128
    lines = chips * micro * local
    pairs = chunks // 2
    final = pairs - 1
    s = lax.axis_index("section")
    t = lax.axis_index("tensor")
    chip, core = t // 2, lax.rem(t, 2)
    sibling = chip * 2 + 1 - core
    following = lax.rem(s + 1, sections)
    previous = lax.rem(s + sections - 1, sections)
    others = range(1, chips)

    def ahead(j):
        return lax.rem(chip + j, chips)

    def behind(j):
        return lax.rem(chip + chips - j, chips)

    def across(j):
        return {"tensor": ahead(j) * 2 + 1 - core}

    def deep(part):
        return slice(0, cut) if part == 0 else slice(cut, depth)

    def span(start, count):
        return pl.ds(pl.multiple_of(start * piece, piece), count * piece)

    def hidden_copy(j, part, m, d):
        lane = core if (part == 1) == (j == 0) else 1 - core
        first = pl.multiple_of((ahead(j) * 2 + lane) * local, local)
        return pltpu.make_async_copy(
            hidden.at[0, m, pl.ds(first, local), deep(d)], rows.at[j, part, m, :, deep(d)], hidden_sem.at[j, part, m, d]
        )

    def hidden_all(j, d, act):
        for part in range(2):
            for m in range(micro):
                act(hidden_copy(j, part, m, d))

    def slab_copy(k, d):
        slot = lax.rem(k, SLABS)
        return pltpu.make_async_copy(
            weight.at[0, deep(d), span(2 * k, 2)], slab.at[slot, deep(d)], slab_sem.at[slot, d]
        )

    def first_copy(h, d):
        place = slice(h * piece, (h + 1) * piece)
        return pltpu.make_async_copy(weight.at[0, deep(d), place], slab.at[0, deep(d), place], first_sem.at[h, d])

    def qkv_copy(p):
        return pltpu.make_async_copy(projector.at[0, span(4 * p, 4), :], qkv.at[p], qkv_sem.at[p])

    res_copy = pltpu.make_async_copy(residual.at[0], res, res_sem)
    gain_copy = pltpu.make_async_copy(gain_in, gain, gain_sem)

    def carried_copy(u):
        return pltpu.make_async_copy(
            carried.at[core, chip, u], carried_out.at[0, :, :, span(u, 1)], carried_sem.at[u]
        )

    def core_copy(k, j):
        place = pl.ds(2 * k, 2)
        return pltpu.make_async_remote_copy(
            src_ref=core_send.at[j, place], dst_ref=core_recv.at[j, place],
            send_sem=core_ss.at[k, j - 1], recv_sem=core_rs.at[k, j - 1],
            device_id={"tensor": sibling}, device_id_type=MESH,
        )

    def core_half(h, j):
        return pltpu.make_async_remote_copy(
            src_ref=core_send.at[j, h], dst_ref=core_recv.at[j, h],
            send_sem=half_ss.at[h, j - 1], recv_sem=half_rs.at[h, j - 1],
            device_id={"tensor": sibling}, device_id_type=MESH,
        )

    def mine_copy(p):
        place = pl.ds(4 * p, 4)
        return pltpu.make_async_remote_copy(
            src_ref=core_send.at[0, place], dst_ref=core_recv.at[0, place],
            send_sem=mine_ss.at[p], recv_sem=mine_rs.at[p],
            device_id={"tensor": sibling}, device_id_type=MESH,
        )

    def x_part(k, j, place):
        return pltpu.make_async_remote_copy(
            src_ref=x_send.at[j - 1, place], dst_ref=x_recv.at[j - 1, place],
            send_sem=x_ss.at[k, j - 1], recv_sem=x_rs.at[k, j - 1],
            device_id=across(j), device_id_type=MESH,
        )

    def x_copy(k, j):
        return x_part(k, j, pl.ds(2 * k, 2))

    def y_copy(p):
        place = pl.ds(4 * p, 4)
        return pltpu.make_async_remote_copy(
            src_ref=stream.at[place], dst_ref=carried.at[core, chip, place], send_sem=y_ss.at[p], recv_sem=y_rs.at[p],
            device_id={"section": following}, device_id_type=MESH,
        )

    def pair(p):
        return (p, 4 * p, 4)

    ends = [(final, 4 * final, 2), (final + 1, 4 * final + 2, 1), (final + 2, 4 * final + 3, 1)]

    def gather_copy(load, j, block):
        n, start, count = load
        place = carried.at[core, block, pl.ds(start, count)]
        return pltpu.make_async_remote_copy(
            src_ref=place, dst_ref=place, send_sem=g_ss.at[n, j - 1], recv_sem=g_rs.at[n, j - 1],
            device_id=across(j), device_id_type=MESH,
        )

    def gathered(load, j):
        n, start, count = load
        place = carried.at[1 - core, behind(j), pl.ds(start, count)]
        return pltpu.make_async_remote_copy(
            src_ref=place, dst_ref=place, send_sem=g_ss.at[n, j - 1], recv_sem=g_rs.at[n, j - 1],
            device_id=across(j), device_id_type=MESH,
        )

    def pass_copy(load, j, lane):
        n, start, count = load
        place = carried.at[lane, behind(j), pl.ds(start, count)]
        return pltpu.make_async_remote_copy(
            src_ref=place, dst_ref=place, send_sem=c_ss.at[n, j], recv_sem=c_rs.at[n, j],
            device_id={"tensor": sibling}, device_id_type=MESH,
        )

    def pass_out(load, j):
        return pass_copy(load, j, core if j == 0 else 1 - core)

    def pass_in(load, j):
        return pass_copy(load, j, 1 - core if j == 0 else core)

    for d in range(2):
        for j in others:
            hidden_all(j, d, lambda copy: copy.start())
        first_copy(0, d).start()

    barrier = pltpu.get_barrier_semaphore()
    pl.semaphore_signal(barrier, inc=1, device_id={"tensor": sibling}, device_id_type=MESH)
    for j in others:
        pl.semaphore_signal(barrier, inc=1, device_id=across(j), device_id_type=MESH)
    pl.semaphore_signal(barrier, inc=1, device_id={"section": following}, device_id_type=MESH)
    if sections > 2:
        pl.semaphore_signal(barrier, inc=1, device_id={"section": previous}, device_id_type=MESH)

    acc[...] = jnp.zeros_like(acc)
    squares[...] = jnp.zeros_like(squares)

    def multiply(j, d, right):
        left = rows[j, :, :, :, d].reshape(2 * micro * local, -1)
        return jnp.dot(left, right, preferred_element_type=F32).reshape(2, micro, local, -1)

    def first_half(h, d):
        return slab[0, deep(d), h * piece:(h + 1) * piece]

    def first_product(h):
        for j in others:
            value = own[j - 1, h] + multiply(j, deep(1), first_half(h, 1))
            core_send[j, h] = value[0].astype(BF16)
            own[j - 1, h] = value

    for j in others:
        hidden_all(j, 0, lambda copy: copy.wait())
    first_copy(0, 0).wait()
    for d in range(2):
        first_copy(1, d).start()
    for j in others:
        own[j - 1, 0] = multiply(j, deep(0), first_half(0, 0))
    for j in others:
        hidden_all(j, 1, lambda copy: copy.wait())
    first_copy(0, 1).wait()
    for d in range(2):
        slab_copy(1, d).start()
    for d in range(2):
        hidden_all(0, d, lambda copy: copy.start())
    first_product(0)
    pl.semaphore_wait(barrier, chips + (2 if sections > 2 else 1))
    for j in others:
        core_half(0, j).start()
    first_copy(1, 0).wait()
    for j in others:
        own[j - 1, 1] = multiply(j, deep(0), first_half(1, 0))
    first_copy(1, 1).wait()
    for k in range(2, SLABS):
        for d in range(2):
            slab_copy(k, d).start()
    first_product(1)
    for j in others:
        core_half(1, j).start()

    def first_send(h):
        for j in others:
            core_half(h, j).wait_recv()
            x_send[j - 1, h] = (own[j - 1, h, 1] + core_recv[j, h].astype(F32)).astype(BF16)
            x_part(0, j, h).start()

    first_send(0)
    res_copy.start()
    gain_copy.start()

    def side_lane(side, c):
        return jnp.where(c == chip, core, 1 - core) if side == 0 else jnp.where(c == chip, 1 - core, core)

    def project(load, side, right):
        _, start, count = load
        values = []
        for n in range(count):
            blocks = [carried[side_lane(side, c), c, start + n].reshape(micro * local, piece) for c in range(chips)]
            values.append(jnp.concatenate(blocks, axis=0).astype(F32))
        values = values[0] if count == 1 else jnp.concatenate(values, axis=-1)
        squared = values * values
        part = squared[:, :128]
        for first in range(128, count * piece, 128):
            part = part + squared[:, first:first + 128]
        squares[side] += part
        scaled = (values * gain[:, span(start, count)]).astype(BF16)
        acc[side] += jnp.dot(scaled, right, preferred_element_type=F32)

    def finish(side):
        mean = jnp.sum(squares[side], axis=-1, keepdims=True) * (1.0 / features)
        value = (acc[side] * lax.rsqrt(mean + 1e-05)).astype(BF16).reshape(chips, micro, local, -1)
        for c in range(chips):
            first = pl.multiple_of((c * 2 + side_lane(side, c)) * local, local)
            for m in range(micro):
                projected_out[0, m, pl.ds(first, local), :] = value[c, m]

    def hand(p, loads):
        y_copy(p).wait_recv()
        for load in loads:
            for j in others:
                gather_copy(load, j, chip).start()
        for load in loads:
            pass_out(load, 0).start()
        for n in range(4):
            carried_copy(4 * p + n).start()

    def relay(load):
        for j in others:
            gathered(load, j).wait_recv()
            pass_out(load, j).start()

    def relayed(load):
        for j in range(chips):
            pass_in(load, j).wait_recv()

    def step(i, _):
        @pl.when(i < chunks)
        def _():
            slot = lax.rem(i, SLABS)
            for d in range(2):
                slab_copy(i, d).wait()
            for j in others:
                value = multiply(j, slice(None), slab[slot])
                for h in range(2):
                    core_send[j, 2 * i + h] = value[0, ..., h * piece:(h + 1) * piece].astype(BF16)
                core_copy(i, j).start()
                for h in range(2):
                    held[j - 1, h] = value[1, ..., h * piece:(h + 1) * piece]

        @pl.when(i == 1)
        def _():
            first_send(1)
            for d in range(2):
                hidden_all(0, d, lambda copy: copy.wait())

        @pl.when(i <= chunks)
        def _():
            k = i - 1
            value = multiply(0, slice(None), slab[lax.rem(k, SLABS)])
            for h in range(2):
                core_send[0, 2 * k + h] = value[0, ..., h * piece:(h + 1) * piece].astype(BF16)
                base[2 * k + h] = value[1, ..., h * piece:(h + 1) * piece]

            @pl.when(lax.rem(k, 2) == 1)
            def _():
                mine_copy(k // 2).start()

            @pl.when(k + SLABS < chunks)
            def _():
                for d in range(2):
                    slab_copy(k + SLABS, d).start()

        @pl.when(i < chunks)
        def _():
            for j in others:
                core_copy(i, j).wait_recv()
                for h in range(2):
                    x_send[j - 1, 2 * i + h] = (held[j - 1, h] + core_recv[j, 2 * i + h].astype(F32)).astype(BF16)
                x_copy(i, j).start()

        k_sum = i - LAG_SUM

        @pl.when((k_sum >= 0) & (k_sum < chunks))
        def _():
            k = k_sum
            p = k // 2

            @pl.when(k == 0)
            def _():
                res_copy.wait()
                gain_copy.wait()

            @pl.when(lax.rem(k, 2) == 0)
            def _():
                qkv_copy(p).start()
                mine_copy(p).wait_recv()

            for j in others:
                x_copy(k, j).wait_recv()
            for h in range(2):
                u = 2 * k + h
                value = base[u] + core_recv[0, u].astype(F32)
                for j in others:
                    value = value + x_recv[j - 1, u].astype(F32)
                stream[u] = (value + res[:, :, span(u, 1)].astype(F32)).astype(BF16)

            @pl.when(lax.rem(k, 2) == 1)
            def _():
                y_copy(p).start()

        k_hand = i - LAG_HAND

        @pl.when((k_hand >= 0) & (lax.rem(k_hand, 2) == 0))
        def _():
            hand(k_hand // 2, [pair(k_hand // 2)])

        return 0

    stop = chunks + LAG_SUM
    lax.fori_loop(1, stop, step, 0)
    begun = (stop - 1 - LAG_HAND) // 2 + 1
    for p in range(begun, final):
        hand(p, [pair(p)])

    def work(p, _):
        relay(pair(p))

        @pl.when(p == 0)
        def _():
            for q in range(pairs):
                qkv_copy(q).wait()

        project(pair(p), 0, qkv[p])

        @pl.when(p == 0)
        def _():
            hand(final, ends)

        relayed(pair(p))
        project(pair(p), 1, qkv[p])
        return 0

    lax.fori_loop(0, final, work, 0)

    def right(load):
        first = (load[1] - 4 * final) * piece
        return qkv[final, first:first + load[2] * piece]

    for load in ends:
        relay(load)
        project(load, 0, right(load))
    finish(0)
    for load in ends:
        relayed(load)
        project(load, 1, right(load))
    finish(1)

    def sent(load):
        pass_out(load, 0).wait_send()
        for j in others:
            gather_copy(load, j, chip).wait_send()
            pass_out(load, j).wait_send()

    def drain(k, _):
        for j in others:
            core_copy(k, j).wait_send()
            x_copy(k, j).wait_send()
        return 0

    def drain_pair(p, _):
        mine_copy(p).wait_send()
        y_copy(p).wait_send()
        for n in range(4):
            carried_copy(4 * p + n).wait()

        @pl.when(p < final)
        def _():
            sent(pair(p))

        return 0

    for j in others:
        for h in range(2):
            core_half(h, j).wait_send()
        x_copy(0, j).wait_send()
    lax.fori_loop(1, chunks, drain, 0)
    lax.fori_loop(0, pairs, drain_pair, 0)
    for load in ends:
        sent(load)


def leave(carried_in, projected_in, carried_out, projected_out, sems):
    copies = [
        pltpu.make_async_copy(carried_in, carried_out, sems.at[0]),
        pltpu.make_async_copy(projected_in, projected_out, sems.at[1]),
    ]
    for copy in copies:
        copy.start()
    for copy in copies:
        copy.wait()


def per_device(sections, tensor, hidden, down_weight, residual, norm_gain, qkv_weight):
    _, micro, tokens, depth = hidden.shape
    local, features = residual.shape[2:]
    outputs = qkv_weight.shape[2]
    chips = tensor // 2
    chunks = CHUNKS
    width = features // chunks
    piece = width // 2
    units, pairs = 2 * chunks, chunks // 2
    dma = pltpu.SemaphoreType.DMA
    anywhere = pl.BlockSpec(memory_space=pl.ANY)
    carried_shape = (1, micro, local, features)
    projected_shape = (1, micro, tokens, outputs)
    results = pl.pallas_call(
        functools.partial(kernel, sections, tensor),
        out_shape=(pltpu.VMEM(carried_shape, BF16), pltpu.VMEM(projected_shape, BF16)),
        in_specs=[pl.BlockSpec(memory_space=pltpu.HBM)] * 5,
        out_specs=(pl.BlockSpec(memory_space=pltpu.VMEM),) * 2,
        scratch_shapes=[
            pltpu.VMEM((chips, 2, micro, local, depth), BF16),
            pltpu.VMEM((SLABS, depth, width), BF16),
            pltpu.VMEM((pairs, 2 * width, outputs), BF16),
            pltpu.VMEM((micro, local, features), BF16),
            pltpu.VMEM((1, features), F32),
            pltpu.VMEM((chips - 1, 2, 2, micro, local, piece), F32),
            pltpu.VMEM((chips - 1, 2, micro, local, piece), F32),
            pltpu.VMEM((chips, units, micro, local, piece), BF16),
            pltpu.VMEM((chips, units, micro, local, piece), BF16),
            pltpu.VMEM((chips - 1, units, micro, local, piece), BF16),
            pltpu.VMEM((chips - 1, units, micro, local, piece), BF16),
            pltpu.VMEM((units, micro, local, piece), F32),
            pltpu.VMEM((units, micro, local, piece), BF16),
            pltpu.VMEM((2, chips, units, micro, local, piece), BF16),
            pltpu.VMEM((2, micro * tokens // 2, outputs), F32),
            pltpu.VMEM((2, micro * tokens // 2, 128), F32),
            dma((chips, 2, micro, 2)), dma((SLABS, 2)), dma((2, 2)), dma((pairs,)), dma, dma, dma((units,)),
            dma((chunks, chips - 1)), dma((chunks, chips - 1)), dma((2, chips - 1)), dma((2, chips - 1)),
            dma((pairs,)), dma((pairs,)),
            dma((chunks, chips - 1)), dma((chunks, chips - 1)),
            dma((pairs,)), dma((pairs,)),
            dma((pairs + 2, chips - 1)), dma((pairs + 2, chips - 1)),
            dma((pairs + 2, chips)), dma((pairs + 2, chips)),
        ],
        compiler_params=pltpu.CompilerParams(
            collective_id=0, has_side_effects=True, vmem_limit_bytes=52 * 1024 * 1024
        ),
    )(
        hidden,
        down_weight,
        pltpu.with_memory_space_constraint(residual, pltpu.HBM),
        pltpu.with_memory_space_constraint(norm_gain, pltpu.HBM),
        qkv_weight,
    )
    return pl.pallas_call(
        leave,
        out_shape=(
            jax.ShapeDtypeStruct(carried_shape, BF16),
            jax.ShapeDtypeStruct(projected_shape, BF16),
        ),
        in_specs=[anywhere] * 2,
        out_specs=(anywhere,) * 2,
        scratch_shapes=[dma((2,))],
    )(*(pltpu.with_memory_space_constraint(x, pltpu.VMEM) for x in results))


def solution(mesh):
    placed = (
        P("section", "dp", None, "tensor"),
        P("section", "tensor", None),
        P("section", "dp", "tensor", None),
        P("section", None),
        P("section", None, "tensor"),
    )
    return jax.shard_map(
        functools.partial(per_device, mesh.shape["section"], mesh.shape["tensor"]),
        mesh=mesh,
        in_specs=placed,
        out_specs=(P("section", "dp", "tensor", None), P("section", "dp", None, "tensor")),
        check_vma=False,
    )
```

```python
import functools

import jax
import jax.numpy as jnp
from jax import lax
from jax.experimental import pallas as pl
from jax.experimental.pallas import tpu as pltpu
from jax.sharding import PartitionSpec as P

MESH = pl.DeviceIdType.MESH
F32 = jnp.float32
BF16 = jnp.bfloat16
CHUNKS = 8
SLABS = 3
LAG_SUM, LAG_HAND = 3, 7


def lane_of(side, c, chip, core):
    return jnp.where(c == chip, core, 1 - core) if side == 0 else jnp.where(c == chip, 1 - core, core)


def kernel(
    sections, tensor, hidden, weight, residual, gain_in, projector,
    carried_out, near_out, far_acc, far_last, far_scale, right_out,
    rows, slab, qkv, res, gain, own, held, core_send, core_recv, x_send, x_recv, base, stream, carried, near_acc, squares,
    hidden_sem, slab_sem, first_sem, qkv_sem, right_sem, res_sem, gain_sem, carried_sem,
    core_ss, core_rs, mine_rs, x_ss, x_rs, y_ss, y_rs, g_ss, g_rs, c_ss, c_rs,
):
    chips = tensor // 2
    units, micro, local, piece = stream.shape
    chunks = units // 2
    width = 2 * piece
    features = units * piece
    depth = rows.shape[-1]
    cut = pl.cdiv(depth // 2, 128) * 128
    lines = chips * micro * local
    pairs = chunks // 2
    final = pairs - 1
    s = lax.axis_index("section")
    t = lax.axis_index("tensor")
    chip, core = t // 2, lax.rem(t, 2)
    sibling = chip * 2 + 1 - core
    following = lax.rem(s + 1, sections)
    previous = lax.rem(s + sections - 1, sections)
    others = range(1, chips)

    def ahead(j):
        return lax.rem(chip + j, chips)

    def behind(j):
        return lax.rem(chip + chips - j, chips)

    def across(j):
        return {"tensor": ahead(j) * 2 + 1 - core}

    def deep(part):
        return slice(0, cut) if part == 0 else slice(cut, depth)

    def span(start, count):
        return pl.ds(pl.multiple_of(start * piece, piece), count * piece)

    def hidden_copy(j, part, m, d):
        lane = core if (part == 1) == (j == 0) else 1 - core
        first = pl.multiple_of((ahead(j) * 2 + lane) * local, local)
        return pltpu.make_async_copy(
            hidden.at[0, m, pl.ds(first, local), deep(d)], rows.at[j, part, m, :, deep(d)], hidden_sem.at[j, d]
        )

    def hidden_start(j, d):
        for part in range(2):
            for m in range(micro):
                hidden_copy(j, part, m, d).start()

    def all_of(ref, sem):
        return pltpu.make_async_copy(ref, ref, sem)

    def hidden_wait(j, d):
        all_of(rows.at[j, :, :, :, deep(d)], hidden_sem.at[j, d]).wait()

    def slab_copy(k, d):
        slot = lax.rem(k, SLABS)
        return pltpu.make_async_copy(
            weight.at[0, deep(d), span(2 * k, 2)], slab.at[slot, deep(d)], slab_sem.at[slot, d]
        )

    def first_copy(h, d):
        place = slice(h * piece, (h + 1) * piece)
        sem = first_sem.at[d] if h == 0 else slab_sem.at[0, d]
        return pltpu.make_async_copy(weight.at[0, deep(d), place], slab.at[0, deep(d), place], sem)

    def qkv_copy(p):
        place = span(4 * p, 4)
        return pltpu.make_async_copy(projector.at[0, place, :], qkv.at[place], qkv_sem)

    right_copy = pltpu.make_async_copy(projector.at[0, features - piece:, :], right_out, right_sem)

    res_copy = pltpu.make_async_copy(residual.at[0], res, res_sem)
    gain_copy = pltpu.make_async_copy(gain_in, gain, gain_sem)

    def carried_copy(u):
        return pltpu.make_async_copy(
            carried.at[core, chip, u], carried_out.at[0, :, :, span(u, 1)], carried_sem
        )

    def core_copy(k, j):
        place = pl.ds(2 * k, 2)
        return pltpu.make_async_remote_copy(
            src_ref=core_send.at[j, place], dst_ref=core_recv.at[j, place],
            send_sem=core_ss, recv_sem=core_rs.at[2 + lax.rem(k, 2), j - 1],
            device_id={"tensor": sibling}, device_id_type=MESH,
        )

    def core_half(h, j):
        return pltpu.make_async_remote_copy(
            src_ref=core_send.at[j, h], dst_ref=core_recv.at[j, h],
            send_sem=core_ss, recv_sem=core_rs.at[h, j - 1],
            device_id={"tensor": sibling}, device_id_type=MESH,
        )

    def mine_copy(p):
        place = pl.ds(4 * p, 4)
        return pltpu.make_async_remote_copy(
            src_ref=core_send.at[0, place], dst_ref=core_recv.at[0, place],
            send_sem=core_ss, recv_sem=mine_rs.at[p],
            device_id={"tensor": sibling}, device_id_type=MESH,
        )

    def x_part(k, j, place):
        return pltpu.make_async_remote_copy(
            src_ref=x_send.at[j - 1, place], dst_ref=x_recv.at[j - 1, place],
            send_sem=x_ss, recv_sem=x_rs.at[k, j - 1],
            device_id=across(j), device_id_type=MESH,
        )

    def x_copy(k, j):
        return x_part(k, j, pl.ds(2 * k, 2))

    def y_copy(p):
        place = pl.ds(4 * p, 4)
        return pltpu.make_async_remote_copy(
            src_ref=stream.at[place], dst_ref=carried.at[core, chip, place], send_sem=y_ss, recv_sem=y_rs.at[p],
            device_id={"section": following}, device_id_type=MESH,
        )

    def pair(p):
        return (p, 4 * p, 4)

    ends = [(final, 4 * final, 2), (final + 1, 4 * final + 2, 1), (final + 2, 4 * final + 3, 1)]

    def gather_copy(load, j, block):
        n, start, count = load
        place = carried.at[core, block, pl.ds(start, count)]
        return pltpu.make_async_remote_copy(
            src_ref=place, dst_ref=place, send_sem=g_ss.at[j - 1], recv_sem=g_rs.at[n, j - 1],
            device_id=across(j), device_id_type=MESH,
        )

    def gathered(load, j):
        n, start, count = load
        place = carried.at[1 - core, behind(j), pl.ds(start, count)]
        return pltpu.make_async_remote_copy(
            src_ref=place, dst_ref=place, send_sem=g_ss.at[j - 1], recv_sem=g_rs.at[n, j - 1],
            device_id=across(j), device_id_type=MESH,
        )

    def pass_out(load, j):
        n, start, count = load
        place = carried.at[core if j == 0 else 1 - core, behind(j), pl.ds(start, count)]
        return pltpu.make_async_remote_copy(
            src_ref=place, dst_ref=place, send_sem=c_ss.at[j], recv_sem=c_rs.at[n],
            device_id={"tensor": sibling}, device_id_type=MESH,
        )

    for d in range(2):
        for j in others:
            hidden_start(j, d)
        first_copy(0, d).start()

    barrier = pltpu.get_barrier_semaphore()
    pl.semaphore_signal(barrier, inc=1, device_id={"tensor": sibling}, device_id_type=MESH)
    for j in others:
        pl.semaphore_signal(barrier, inc=1, device_id=across(j), device_id_type=MESH)
    pl.semaphore_signal(barrier, inc=1, device_id={"section": following}, device_id_type=MESH)
    if sections > 2:
        pl.semaphore_signal(barrier, inc=1, device_id={"section": previous}, device_id_type=MESH)

    acc = (near_acc, far_acc)
    for ref in acc:
        ref[...] = jnp.zeros_like(ref)
    squares[...] = jnp.zeros_like(squares)

    def multiply(j, d, right):
        left = rows[j, :, :, :, d].reshape(2 * micro * local, -1)
        return jnp.dot(left, right, preferred_element_type=F32).reshape(2, micro, local, -1)

    def first_half(h, d):
        return slab[0, deep(d), h * piece:(h + 1) * piece]

    def first_product(h):
        for j in others:
            value = own[j - 1, h] + multiply(j, deep(1), first_half(h, 1))
            core_send[j, h] = value[0].astype(BF16)
            own[j - 1, h] = value

    for j in others:
        hidden_wait(j, 0)
    first_copy(0, 0).wait()
    for d in range(2):
        first_copy(1, d).start()
    for j in others:
        own[j - 1, 0] = multiply(j, deep(0), first_half(0, 0))
    for j in others:
        hidden_wait(j, 1)
    first_copy(0, 1).wait()
    for d in range(2):
        slab_copy(1, d).start()
    for d in range(2):
        hidden_start(0, d)
    first_product(0)
    pl.semaphore_wait(barrier, chips + (2 if sections > 2 else 1))
    for j in others:
        core_half(0, j).start()
    first_copy(1, 0).wait()
    for j in others:
        own[j - 1, 1] = multiply(j, deep(0), first_half(1, 0))
    first_copy(1, 1).wait()
    for k in range(2, SLABS):
        for d in range(2):
            slab_copy(k, d).start()
    first_product(1)
    for j in others:
        core_half(1, j).start()

    def first_send(h):
        for j in others:
            core_half(h, j).wait_recv()
            x_send[j - 1, h] = (own[j - 1, h, 1] + core_recv[j, h].astype(F32)).astype(BF16)
            x_part(0, j, h).start()

    first_send(0)
    res_copy.start()
    gain_copy.start()

    def side_lane(side, c):
        return lane_of(side, c, chip, core)

    def scaled(load, side):
        _, start, count = load
        values = []
        for n in range(count):
            blocks = [carried[side_lane(side, c), c, start + n].reshape(micro * local, piece) for c in range(chips)]
            values.append(jnp.concatenate(blocks, axis=0).astype(F32))
        values = values[0] if count == 1 else jnp.concatenate(values, axis=-1)
        squared = values * values
        part = squared[:, :128]
        for first in range(128, count * piece, 128):
            part = part + squared[:, first:first + 128]
        squares[side] += part
        return (values * gain[:, span(start, count)]).astype(BF16)

    def project(load, side):
        _, start, count = load
        acc[side][...] += jnp.dot(scaled(load, side), qkv[span(start, count)], preferred_element_type=F32)

    def scale(side):
        mean = jnp.sum(squares[side], axis=-1, keepdims=True) * (1.0 / features)
        return lax.rsqrt(mean + 1e-05)

    def hand(p, loads):
        y_copy(p).wait_recv()
        for load in loads:
            for j in others:
                gather_copy(load, j, chip).start()
        for load in loads:
            pass_out(load, 0).start()
        for n in range(4):
            carried_copy(4 * p + n).start()

    def relay(load):
        for j in others:
            gathered(load, j).wait_recv()
            pass_out(load, j).start()

    def relayed(load):
        n, start, count = load
        all_of(carried.at[core, :, pl.ds(start, count)], c_rs.at[n]).wait()

    def step(i, _):
        @pl.when(i < chunks)
        def _():
            slot = lax.rem(i, SLABS)
            for d in range(2):
                slab_copy(i, d).wait()
            for j in others:
                value = multiply(j, slice(None), slab[slot])
                for h in range(2):
                    core_send[j, 2 * i + h] = value[0, ..., h * piece:(h + 1) * piece].astype(BF16)
                core_copy(i, j).start()
                for h in range(2):
                    held[j - 1, h] = value[1, ..., h * piece:(h + 1) * piece]

        @pl.when(i == 1)
        def _():
            first_send(1)
            for d in range(2):
                hidden_wait(0, d)

        @pl.when(i <= chunks)
        def _():
            k = i - 1
            value = multiply(0, slice(None), slab[lax.rem(k, SLABS)])
            for h in range(2):
                core_send[0, 2 * k + h] = value[0, ..., h * piece:(h + 1) * piece].astype(BF16)
                base[2 * k + h] = value[1, ..., h * piece:(h + 1) * piece]

            @pl.when(lax.rem(k, 2) == 1)
            def _():
                mine_copy(k // 2).start()

            @pl.when(k + SLABS < chunks)
            def _():
                for d in range(2):
                    slab_copy(k + SLABS, d).start()

        @pl.when(i < chunks)
        def _():
            for j in others:
                core_copy(i, j).wait_recv()
                for h in range(2):
                    x_send[j - 1, 2 * i + h] = (held[j - 1, h] + core_recv[j, 2 * i + h].astype(F32)).astype(BF16)
                x_copy(i, j).start()

        k_sum = i - LAG_SUM

        @pl.when((k_sum >= 0) & (k_sum < chunks))
        def _():
            k = k_sum
            p = k // 2

            @pl.when(k == 0)
            def _():
                res_copy.wait()
                gain_copy.wait()
                right_copy.start()

            @pl.when(lax.rem(k, 2) == 0)
            def _():
                qkv_copy(p).start()
                mine_copy(p).wait_recv()

            for j in others:
                x_copy(k, j).wait_recv()
            for h in range(2):
                u = 2 * k + h
                value = base[u] + core_recv[0, u].astype(F32)
                for j in others:
                    value = value + x_recv[j - 1, u].astype(F32)
                stream[u] = (value + res[:, :, span(u, 1)].astype(F32)).astype(BF16)

            @pl.when(lax.rem(k, 2) == 1)
            def _():
                y_copy(p).start()

        k_hand = i - LAG_HAND

        @pl.when((k_hand >= 0) & (lax.rem(k_hand, 2) == 0))
        def _():
            hand(k_hand // 2, [pair(k_hand // 2)])

        return 0

    stop = chunks + LAG_SUM
    lax.fori_loop(1, stop, step, 0)
    begun = (stop - 1 - LAG_HAND) // 2 + 1
    for p in range(begun, final):
        hand(p, [pair(p)])

    def work(p, _):
        relay(pair(p))

        @pl.when(p == 0)
        def _():
            all_of(qkv, qkv_sem).wait()

        project(pair(p), 0)

        @pl.when(p == 0)
        def _():
            hand(final, ends)

        relayed(pair(p))
        project(pair(p), 1)
        return 0

    lax.fori_loop(0, final, work, 0)

    for load in ends:
        relay(load)
        project(load, 0)
    near_out[...] = (near_acc[...] * scale(0)).astype(BF16)
    for load in ends[:-1]:
        relayed(load)
        project(load, 1)
    right_copy.wait()
    relayed(ends[-1])
    far_last[...] = scaled(ends[-1], 1)
    far_scale[...] = jnp.broadcast_to(scale(1), far_scale.shape)

    all_of(core_send, core_ss).wait()
    all_of(x_send, x_ss).wait()
    all_of(stream, y_ss).wait()
    all_of(carried_out.at[0], carried_sem).wait()
    all_of(carried.at[core, chip], c_ss.at[0]).wait()
    for j in others:
        all_of(carried.at[core, chip], g_ss.at[j - 1]).wait()
        all_of(carried.at[1 - core, behind(j)], c_ss.at[j]).wait()


def leave(
    tensor, carried_in, near_in, far_acc, far_last, far_scale, right, carried_out, projected_out,
    far, carried_sem, near_sem, far_sem,
):
    chips = tensor // 2
    micro, local = carried_in.shape[1:3]
    t = lax.axis_index("tensor")
    chip, core = t // 2, lax.rem(t, 2)
    carried_copy = pltpu.make_async_copy(carried_in, carried_out, carried_sem)

    def out_copies(ref, side, sem):
        copies = []
        for c in range(chips):
            first = pl.multiple_of((c * 2 + lane_of(side, c, chip, core)) * local, local)
            for m in range(micro):
                lines = pl.ds((c * micro + m) * local, local)
                copies.append(pltpu.make_async_copy(
                    ref.at[lines], projected_out.at[0, m, pl.ds(first, local), :], sem.at[c, m]
                ))
        return copies

    near_copies = out_copies(near_in, 0, near_sem)
    far_copies = out_copies(far, 1, far_sem)
    carried_copy.start()
    for copy in near_copies:
        copy.start()
    for c in range(chips):
        lines = slice(c * micro * local, (c + 1) * micro * local)
        value = far_acc[lines] + jnp.dot(far_last[lines], right[...], preferred_element_type=F32)
        far[lines] = (value * far_scale[lines, :1]).astype(BF16)
        for m in range(micro):
            far_copies[c * micro + m].start()
    for copy in [carried_copy] + near_copies + far_copies:
        copy.wait()


def per_device(sections, tensor, hidden, down_weight, residual, norm_gain, qkv_weight):
    _, micro, tokens, depth = hidden.shape
    local, features = residual.shape[2:]
    outputs = qkv_weight.shape[2]
    chips = tensor // 2
    chunks = CHUNKS
    width = features // chunks
    piece = width // 2
    units, pairs = 2 * chunks, chunks // 2
    dma = pltpu.SemaphoreType.DMA
    anywhere = pl.BlockSpec(memory_space=pl.ANY)
    carried_shape = (1, micro, local, features)
    projected_shape = (1, micro, tokens, outputs)
    lines = micro * tokens // 2
    results = pl.pallas_call(
        functools.partial(kernel, sections, tensor),
        out_shape=(
            pltpu.VMEM(carried_shape, BF16),
            pltpu.VMEM((lines, outputs), BF16),
            pltpu.VMEM((lines, outputs), F32),
            pltpu.VMEM((lines, piece), BF16),
            pltpu.VMEM((lines, 128), F32),
            pltpu.VMEM((piece, outputs), BF16),
        ),
        in_specs=[pl.BlockSpec(memory_space=pltpu.HBM)] * 5,
        out_specs=(pl.BlockSpec(memory_space=pltpu.VMEM),) * 6,
        scratch_shapes=[
            pltpu.VMEM((chips, 2, micro, local, depth), BF16),
            pltpu.VMEM((SLABS, depth, width), BF16),
            pltpu.VMEM((features, outputs), BF16),
            pltpu.VMEM((micro, local, features), BF16),
            pltpu.VMEM((1, features), F32),
            pltpu.VMEM((chips - 1, 2, 2, micro, local, piece), F32),
            pltpu.VMEM((chips - 1, 2, micro, local, piece), F32),
            pltpu.VMEM((chips, units, micro, local, piece), BF16),
            pltpu.VMEM((chips, units, micro, local, piece), BF16),
            pltpu.VMEM((chips - 1, units, micro, local, piece), BF16),
            pltpu.VMEM((chips - 1, units, micro, local, piece), BF16),
            pltpu.VMEM((units, micro, local, piece), F32),
            pltpu.VMEM((units, micro, local, piece), BF16),
            pltpu.VMEM((2, chips, units, micro, local, piece), BF16),
            pltpu.VMEM((lines, outputs), F32),
            pltpu.VMEM((2, lines, 128), F32),
            dma((chips, 2)), dma((SLABS, 2)), dma((2,)), dma, dma, dma, dma, dma,
            dma, dma((4, chips - 1)), dma((pairs,)), dma, dma((chunks, chips - 1)), dma, dma((pairs,)),
            dma((chips - 1,)), dma((pairs + 2, chips - 1)), dma((chips,)), dma((pairs + 2,)),
        ],
        compiler_params=pltpu.CompilerParams(
            collective_id=0, has_side_effects=True, vmem_limit_bytes=50 * 1024 * 1024
        ),
    )(
        hidden,
        down_weight,
        pltpu.with_memory_space_constraint(residual, pltpu.HBM),
        pltpu.with_memory_space_constraint(norm_gain, pltpu.HBM),
        qkv_weight,
    )
    return pl.pallas_call(
        functools.partial(leave, tensor),
        out_shape=(
            jax.ShapeDtypeStruct(carried_shape, BF16),
            jax.ShapeDtypeStruct(projected_shape, BF16),
        ),
        in_specs=[pl.BlockSpec(memory_space=pltpu.VMEM)] * 6,
        out_specs=(anywhere,) * 2,
        scratch_shapes=[pltpu.VMEM((lines, outputs), BF16), dma, dma((chips, micro)), dma((chips, micro))],
        compiler_params=pltpu.CompilerParams(vmem_limit_bytes=8 * 1024 * 1024),
    )(*(pltpu.with_memory_space_constraint(x, pltpu.VMEM) for x in results))


def solution(mesh):
    placed = (
        P("section", "dp", None, "tensor"),
        P("section", "tensor", None),
        P("section", "dp", "tensor", None),
        P("section", None),
        P("section", None, "tensor"),
    )
    return jax.shard_map(
        functools.partial(per_device, mesh.shape["section"], mesh.shape["tensor"]),
        mesh=mesh,
        in_specs=placed,
        out_specs=(P("section", "dp", "tensor", None), P("section", "dp", None, "tensor")),
        check_vma=False,
    )
```

```python
import functools

import jax
import jax.numpy as jnp
from jax import lax
from jax.experimental import pallas as pl
from jax.experimental.pallas import tpu as pltpu
from jax.sharding import PartitionSpec as P

MESH = pl.DeviceIdType.MESH
F32 = jnp.float32
BF16 = jnp.bfloat16
CHUNKS = 8
SLABS = 3
LAG_SUM, LAG_HAND = 3, 9


def lane_of(side, c, chip, core):
    return jnp.where(c == chip, core, 1 - core) if side == 0 else jnp.where(c == chip, 1 - core, core)


def kernel(
    sections, tensor, hidden, weight, residual, gain_in, projector,
    carried_out, near_out, far_acc, far_last, far_scale, right_out,
    rows, slab, qkv, res, gain, own, held, core_send, core_recv, x_send, x_recv, base, stream, carried, near_acc, squares,
    hidden_sem, slab_sem, first_sem, qkv_sem, right_sem, res_sem, gain_sem, carried_sem,
    core_ss, core_rs, mine_rs, x_ss, x_rs, y_ss, y_rs, g_ss, g_rs, c_ss, c_rs,
):
    chips = tensor // 2
    units, micro, local, piece = stream.shape
    chunks = units // 2
    width = 2 * piece
    features = units * piece
    depth = rows.shape[-1]
    cut = pl.cdiv(depth // 2, 128) * 128
    lines = chips * micro * local
    pairs = chunks // 2
    final = pairs - 1
    s = lax.axis_index("section")
    t = lax.axis_index("tensor")
    chip, core = t // 2, lax.rem(t, 2)
    sibling = chip * 2 + 1 - core
    following = lax.rem(s + 1, sections)
    previous = lax.rem(s + sections - 1, sections)
    others = range(1, chips)

    def ahead(j):
        return lax.rem(chip + j, chips)

    def behind(j):
        return lax.rem(chip + chips - j, chips)

    def across(j):
        return {"tensor": ahead(j) * 2 + 1 - core}

    def deep(part):
        return slice(0, cut) if part == 0 else slice(cut, depth)

    def span(start, count):
        return pl.ds(pl.multiple_of(start * piece, piece), count * piece)

    def hidden_copy(j, part, m, d):
        lane = core if (part == 1) == (j == 0) else 1 - core
        first = pl.multiple_of((ahead(j) * 2 + lane) * local, local)
        return pltpu.make_async_copy(
            hidden.at[0, m, pl.ds(first, local), deep(d)], rows.at[j, part, m, :, deep(d)], hidden_sem.at[j, d]
        )

    def hidden_start(j, d):
        for part in range(2):
            for m in range(micro):
                hidden_copy(j, part, m, d).start()

    def all_of(ref, sem):
        return pltpu.make_async_copy(ref, ref, sem)

    def hidden_wait(j, d):
        all_of(rows.at[j, :, :, :, deep(d)], hidden_sem.at[j, d]).wait()

    def slab_copy(k, d):
        slot = lax.rem(k, SLABS)
        return pltpu.make_async_copy(
            weight.at[0, deep(d), span(2 * k, 2)], slab.at[slot, deep(d)], slab_sem.at[slot, d]
        )

    def first_copy(h, d):
        place = slice(h * piece, (h + 1) * piece)
        sem = first_sem.at[d] if h == 0 else slab_sem.at[0, d]
        return pltpu.make_async_copy(weight.at[0, deep(d), place], slab.at[0, deep(d), place], sem)

    def qkv_copy(p):
        place = span(4 * p, 4)
        return pltpu.make_async_copy(projector.at[0, place, :], qkv.at[place], qkv_sem)

    right_copy = pltpu.make_async_copy(projector.at[0, features - piece:, :], right_out, right_sem)

    res_copy = pltpu.make_async_copy(residual.at[0], res, res_sem)
    gain_copy = pltpu.make_async_copy(gain_in, gain, gain_sem)

    def carried_copy(u):
        return pltpu.make_async_copy(
            carried.at[core, chip, u], carried_out.at[0, :, :, span(u, 1)], carried_sem
        )

    def core_copy(k, j):
        place = pl.ds(2 * k, 2)
        return pltpu.make_async_remote_copy(
            src_ref=core_send.at[j, place], dst_ref=core_recv.at[j, place],
            send_sem=core_ss, recv_sem=core_rs.at[2 + lax.rem(k, 2), j - 1],
            device_id={"tensor": sibling}, device_id_type=MESH,
        )

    def core_half(h, j):
        return pltpu.make_async_remote_copy(
            src_ref=core_send.at[j, h], dst_ref=core_recv.at[j, h],
            send_sem=core_ss, recv_sem=core_rs.at[h, j - 1],
            device_id={"tensor": sibling}, device_id_type=MESH,
        )

    def mine_copy(p):
        place = pl.ds(4 * p, 4)
        return pltpu.make_async_remote_copy(
            src_ref=core_send.at[0, place], dst_ref=core_recv.at[0, place],
            send_sem=core_ss, recv_sem=mine_rs.at[p],
            device_id={"tensor": sibling}, device_id_type=MESH,
        )

    def x_part(k, j, place):
        return pltpu.make_async_remote_copy(
            src_ref=x_send.at[j - 1, place], dst_ref=x_recv.at[j - 1, place],
            send_sem=x_ss, recv_sem=x_rs.at[k, j - 1],
            device_id=across(j), device_id_type=MESH,
        )

    def x_copy(k, j):
        return x_part(k, j, pl.ds(2 * k, 2))

    def y_copy(p):
        place = pl.ds(4 * p, 4)
        return pltpu.make_async_remote_copy(
            src_ref=stream.at[place], dst_ref=carried.at[core, chip, place], send_sem=y_ss, recv_sem=y_rs.at[p],
            device_id={"section": following}, device_id_type=MESH,
        )

    def pair(p):
        return (p, 4 * p, 4)

    ends = [(final, 4 * final, 2), (final + 1, 4 * final + 2, 1), (final + 2, 4 * final + 3, 1)]

    def gather_copy(load, j, block):
        n, start, count = load
        place = carried.at[core, block, pl.ds(start, count)]
        return pltpu.make_async_remote_copy(
            src_ref=place, dst_ref=place, send_sem=g_ss.at[j - 1], recv_sem=g_rs.at[n, j - 1],
            device_id=across(j), device_id_type=MESH,
        )

    def gathered(load, j):
        n, start, count = load
        place = carried.at[1 - core, behind(j), pl.ds(start, count)]
        return pltpu.make_async_remote_copy(
            src_ref=place, dst_ref=place, send_sem=g_ss.at[j - 1], recv_sem=g_rs.at[n, j - 1],
            device_id=across(j), device_id_type=MESH,
        )

    def pass_out(load, j):
        n, start, count = load
        place = carried.at[core if j == 0 else 1 - core, behind(j), pl.ds(start, count)]
        return pltpu.make_async_remote_copy(
            src_ref=place, dst_ref=place, send_sem=c_ss.at[j], recv_sem=c_rs.at[n],
            device_id={"tensor": sibling}, device_id_type=MESH,
        )

    for d in range(2):
        for j in others:
            hidden_start(j, d)
        first_copy(0, d).start()

    barrier = pltpu.get_barrier_semaphore()
    pl.semaphore_signal(barrier, inc=1, device_id={"tensor": sibling}, device_id_type=MESH)
    for j in others:
        pl.semaphore_signal(barrier, inc=1, device_id=across(j), device_id_type=MESH)
    pl.semaphore_signal(barrier, inc=1, device_id={"section": following}, device_id_type=MESH)
    if sections > 2:
        pl.semaphore_signal(barrier, inc=1, device_id={"section": previous}, device_id_type=MESH)

    acc = (near_acc, far_acc)
    for ref in acc:
        ref[...] = jnp.zeros_like(ref)
    squares[...] = jnp.zeros_like(squares)

    def multiply(j, d, right):
        left = rows[j, :, :, :, d].reshape(2 * micro * local, -1)
        return jnp.dot(left, right, preferred_element_type=F32).reshape(2, micro, local, -1)

    def first_half(h, d):
        return slab[0, deep(d), h * piece:(h + 1) * piece]

    def first_product(h):
        for j in others:
            value = own[j - 1, h] + multiply(j, deep(1), first_half(h, 1))
            core_send[j, h] = value[0].astype(BF16)
            own[j - 1, h] = value

    for j in others:
        hidden_wait(j, 0)
    first_copy(0, 0).wait()
    for d in range(2):
        first_copy(1, d).start()
    for j in others:
        own[j - 1, 0] = multiply(j, deep(0), first_half(0, 0))
    for j in others:
        hidden_wait(j, 1)
    first_copy(0, 1).wait()
    for d in range(2):
        slab_copy(1, d).start()
    for d in range(2):
        hidden_start(0, d)
    first_product(0)
    pl.semaphore_wait(barrier, chips + (2 if sections > 2 else 1))
    for j in others:
        core_half(0, j).start()
    first_copy(1, 0).wait()
    for j in others:
        own[j - 1, 1] = multiply(j, deep(0), first_half(1, 0))
    first_copy(1, 1).wait()
    for k in range(2, SLABS):
        for d in range(2):
            slab_copy(k, d).start()
    first_product(1)
    for j in others:
        core_half(1, j).start()

    def first_send(h):
        for j in others:
            core_half(h, j).wait_recv()
            x_send[j - 1, h] = (own[j - 1, h, 1] + core_recv[j, h].astype(F32)).astype(BF16)
            x_part(0, j, h).start()

    first_send(0)
    res_copy.start()
    gain_copy.start()

    def side_lane(side, c):
        return lane_of(side, c, chip, core)

    def scaled(load, side):
        _, start, count = load
        values = []
        for n in range(count):
            blocks = [carried[side_lane(side, c), c, start + n].reshape(micro * local, piece) for c in range(chips)]
            values.append(jnp.concatenate(blocks, axis=0).astype(F32))
        values = values[0] if count == 1 else jnp.concatenate(values, axis=-1)
        squared = values * values
        part = squared[:, :128]
        for first in range(128, count * piece, 128):
            part = part + squared[:, first:first + 128]
        squares[side] += part
        return (values * gain[:, span(start, count)]).astype(BF16)

    def project(load, side):
        _, start, count = load
        acc[side][...] += jnp.dot(scaled(load, side), qkv[span(start, count)], preferred_element_type=F32)

    def scale(side):
        mean = jnp.sum(squares[side], axis=-1, keepdims=True) * (1.0 / features)
        return lax.rsqrt(mean + 1e-05)

    def hand(p, loads):
        y_copy(p).wait_recv()
        for load in loads:
            for j in others:
                gather_copy(load, j, chip).start()
        for load in loads:
            pass_out(load, 0).start()
        for n in range(4):
            carried_copy(4 * p + n).start()

    def relay(load):
        for j in others:
            gathered(load, j).wait_recv()
            pass_out(load, j).start()

    def relayed(load):
        n, start, count = load
        all_of(carried.at[core, :, pl.ds(start, count)], c_rs.at[n]).wait()

    def step(i, _):
        @pl.when(i < chunks)
        def _():
            slot = lax.rem(i, SLABS)
            for d in range(2):
                slab_copy(i, d).wait()
            for j in others:
                value = multiply(j, slice(None), slab[slot])
                for h in range(2):
                    core_send[j, 2 * i + h] = value[0, ..., h * piece:(h + 1) * piece].astype(BF16)
                core_copy(i, j).start()
                for h in range(2):
                    held[j - 1, h] = value[1, ..., h * piece:(h + 1) * piece]

        @pl.when(i == 1)
        def _():
            first_send(1)
            for d in range(2):
                hidden_wait(0, d)

        @pl.when(i <= chunks)
        def _():
            k = i - 1
            value = multiply(0, slice(None), slab[lax.rem(k, SLABS)])
            for h in range(2):
                core_send[0, 2 * k + h] = value[0, ..., h * piece:(h + 1) * piece].astype(BF16)
                base[2 * k + h] = value[1, ..., h * piece:(h + 1) * piece]

            @pl.when(lax.rem(k, 2) == 1)
            def _():
                mine_copy(k // 2).start()

            @pl.when(k + SLABS < chunks)
            def _():
                for d in range(2):
                    slab_copy(k + SLABS, d).start()

        @pl.when(i < chunks)
        def _():
            for j in others:
                core_copy(i, j).wait_recv()
                for h in range(2):
                    x_send[j - 1, 2 * i + h] = (held[j - 1, h] + core_recv[j, 2 * i + h].astype(F32)).astype(BF16)
                x_copy(i, j).start()

        k_sum = i - LAG_SUM

        @pl.when((k_sum >= 0) & (k_sum < chunks))
        def _():
            k = k_sum
            p = k // 2

            @pl.when(k == 0)
            def _():
                res_copy.wait()
                gain_copy.wait()
                right_copy.start()

            @pl.when(lax.rem(k, 2) == 0)
            def _():
                qkv_copy(p).start()
                mine_copy(p).wait_recv()

            for j in others:
                x_copy(k, j).wait_recv()
            for h in range(2):
                u = 2 * k + h
                value = base[u] + core_recv[0, u].astype(F32)
                for j in others:
                    value = value + x_recv[j - 1, u].astype(F32)
                stream[u] = (value + res[:, :, span(u, 1)].astype(F32)).astype(BF16)

            @pl.when(lax.rem(k, 2) == 1)
            def _():
                y_copy(p).start()

        k_hand = i - LAG_HAND

        @pl.when((k_hand >= 0) & (lax.rem(k_hand, 2) == 0))
        def _():
            hand(k_hand // 2, [pair(k_hand // 2)])

        return 0

    stop = chunks + LAG_SUM
    lax.fori_loop(1, stop, step, 0)
    begun = (stop - 1 - LAG_HAND) // 2 + 1
    for p in range(begun, final):
        hand(p, [pair(p)])

    def work(p, _):
        relay(pair(p))

        @pl.when(p == 0)
        def _():
            all_of(qkv, qkv_sem).wait()

        project(pair(p), 0)

        @pl.when(p == 0)
        def _():
            hand(final, ends)

        relayed(pair(p))
        project(pair(p), 1)
        return 0

    lax.fori_loop(0, final, work, 0)

    for load in ends[:-1]:
        relay(load)
        project(load, 0)
    relayed(ends[0])
    project(ends[0], 1)
    right_copy.wait()
    relay(ends[-1])
    relayed(ends[1])
    project(ends[1], 1)
    project(ends[-1], 0)
    near_out[...] = (near_acc[...] * scale(0)).astype(BF16)
    relayed(ends[-1])
    far_last[...] = scaled(ends[-1], 1)
    far_scale[...] = jnp.broadcast_to(scale(1), far_scale.shape)

    all_of(core_send, core_ss).wait()
    all_of(x_send, x_ss).wait()
    all_of(stream, y_ss).wait()
    all_of(carried_out.at[0], carried_sem).wait()
    all_of(carried.at[core, chip], c_ss.at[0]).wait()
    for j in others:
        all_of(carried.at[core, chip], g_ss.at[j - 1]).wait()
        all_of(carried.at[1 - core, behind(j)], c_ss.at[j]).wait()


def leave(
    tensor, carried_in, near_in, far_acc, far_last, far_scale, right, carried_out, projected_out,
    far, carried_sem, near_sem, far_sem,
):
    chips = tensor // 2
    micro, local = carried_in.shape[1:3]
    t = lax.axis_index("tensor")
    chip, core = t // 2, lax.rem(t, 2)
    carried_copy = pltpu.make_async_copy(carried_in, carried_out, carried_sem)

    def out_copies(ref, side, sem):
        copies = []
        for c in range(chips):
            first = pl.multiple_of((c * 2 + lane_of(side, c, chip, core)) * local, local)
            for m in range(micro):
                lines = pl.ds((c * micro + m) * local, local)
                copies.append(pltpu.make_async_copy(
                    ref.at[lines], projected_out.at[0, m, pl.ds(first, local), :], sem.at[c, m]
                ))
        return copies

    near_copies = out_copies(near_in, 0, near_sem)
    far_copies = out_copies(far, 1, far_sem)
    carried_copy.start()
    for copy in near_copies:
        copy.start()
    for c in range(chips):
        lines = slice(c * micro * local, (c + 1) * micro * local)
        value = far_acc[lines] + jnp.dot(far_last[lines], right[...], preferred_element_type=F32)
        far[lines] = (value * far_scale[lines, :1]).astype(BF16)
        for m in range(micro):
            far_copies[c * micro + m].start()
    for copy in [carried_copy] + near_copies + far_copies:
        copy.wait()


def per_device(sections, tensor, hidden, down_weight, residual, norm_gain, qkv_weight):
    _, micro, tokens, depth = hidden.shape
    local, features = residual.shape[2:]
    outputs = qkv_weight.shape[2]
    chips = tensor // 2
    chunks = CHUNKS
    width = features // chunks
    piece = width // 2
    units, pairs = 2 * chunks, chunks // 2
    dma = pltpu.SemaphoreType.DMA
    anywhere = pl.BlockSpec(memory_space=pl.ANY)
    carried_shape = (1, micro, local, features)
    projected_shape = (1, micro, tokens, outputs)
    lines = micro * tokens // 2
    results = pl.pallas_call(
        functools.partial(kernel, sections, tensor),
        out_shape=(
            pltpu.VMEM(carried_shape, BF16),
            pltpu.VMEM((lines, outputs), BF16),
            pltpu.VMEM((lines, outputs), F32),
            pltpu.VMEM((lines, piece), BF16),
            pltpu.VMEM((lines, 128), F32),
            pltpu.VMEM((piece, outputs), BF16),
        ),
        in_specs=[pl.BlockSpec(memory_space=pltpu.HBM)] * 5,
        out_specs=(pl.BlockSpec(memory_space=pltpu.VMEM),) * 6,
        scratch_shapes=[
            pltpu.VMEM((chips, 2, micro, local, depth), BF16),
            pltpu.VMEM((SLABS, depth, width), BF16),
            pltpu.VMEM((features, outputs), BF16),
            pltpu.VMEM((micro, local, features), BF16),
            pltpu.VMEM((1, features), F32),
            pltpu.VMEM((chips - 1, 2, 2, micro, local, piece), F32),
            pltpu.VMEM((chips - 1, 2, micro, local, piece), F32),
            pltpu.VMEM((chips, units, micro, local, piece), BF16),
            pltpu.VMEM((chips, units, micro, local, piece), BF16),
            pltpu.VMEM((chips - 1, units, micro, local, piece), BF16),
            pltpu.VMEM((chips - 1, units, micro, local, piece), BF16),
            pltpu.VMEM((units, micro, local, piece), F32),
            pltpu.VMEM((units, micro, local, piece), BF16),
            pltpu.VMEM((2, chips, units, micro, local, piece), BF16),
            pltpu.VMEM((lines, outputs), F32),
            pltpu.VMEM((2, lines, 128), F32),
            dma((chips, 2)), dma((SLABS, 2)), dma((2,)), dma, dma, dma, dma, dma,
            dma, dma((4, chips - 1)), dma((pairs,)), dma, dma((chunks, chips - 1)), dma, dma((pairs,)),
            dma((chips - 1,)), dma((pairs + 2, chips - 1)), dma((chips,)), dma((pairs + 2,)),
        ],
        compiler_params=pltpu.CompilerParams(
            collective_id=0, has_side_effects=True, vmem_limit_bytes=50 * 1024 * 1024
        ),
    )(
        hidden,
        down_weight,
        pltpu.with_memory_space_constraint(residual, pltpu.HBM),
        pltpu.with_memory_space_constraint(norm_gain, pltpu.HBM),
        qkv_weight,
    )
    return pl.pallas_call(
        functools.partial(leave, tensor),
        out_shape=(
            jax.ShapeDtypeStruct(carried_shape, BF16),
            jax.ShapeDtypeStruct(projected_shape, BF16),
        ),
        in_specs=[pl.BlockSpec(memory_space=pltpu.VMEM)] * 6,
        out_specs=(anywhere,) * 2,
        scratch_shapes=[pltpu.VMEM((lines, outputs), BF16), dma, dma((chips, micro)), dma((chips, micro))],
        compiler_params=pltpu.CompilerParams(vmem_limit_bytes=8 * 1024 * 1024),
    )(*(pltpu.with_memory_space_constraint(x, pltpu.VMEM) for x in results))


def solution(mesh):
    placed = (
        P("section", "dp", None, "tensor"),
        P("section", "tensor", None),
        P("section", "dp", "tensor", None),
        P("section", None),
        P("section", None, "tensor"),
    )
    return jax.shard_map(
        functools.partial(per_device, mesh.shape["section"], mesh.shape["tensor"]),
        mesh=mesh,
        in_specs=placed,
        out_specs=(P("section", "dp", "tensor", None), P("section", "dp", None, "tensor")),
        check_vma=False,
    )
```

```python
import functools

import jax
import jax.numpy as jnp
from jax import lax
from jax.experimental import pallas as pl
from jax.experimental.pallas import tpu as pltpu
from jax.sharding import PartitionSpec as P

MESH = pl.DeviceIdType.MESH
F32 = jnp.float32
BF16 = jnp.bfloat16
CHUNKS = 8
SLABS = 3
LAG_SUM, LAG_HAND = 3, 9


def lane_of(side, c, chip, core):
    return jnp.where(c == chip, core, 1 - core) if side == 0 else jnp.where(c == chip, 1 - core, core)


def kernel(
    sections, tensor, hidden, weight, residual, gain_in, projector,
    carried_out, near_out, far_acc, far_last, far_scale, right_out,
    rows, slab, qkv, res, gain, own, held, core_send, core_recv, x_send, x_recv, base, stream, carried, near_acc, squares,
    hidden_sem, slab_sem, first_sem, qkv_sem, right_sem, res_sem, gain_sem, carried_sem,
    core_ss, core_rs, mine_rs, x_ss, x_rs, y_ss, y_rs, g_ss, g_rs, c_ss, c_rs,
):
    chips = tensor // 2
    units, micro, local, piece = stream.shape
    chunks = units // 2
    width = 2 * piece
    features = units * piece
    depth = rows.shape[-1]
    cut = pl.cdiv(depth // 2, 128) * 128
    lines = chips * micro * local
    pairs = chunks // 2
    final = pairs - 1
    s = lax.axis_index("section")
    t = lax.axis_index("tensor")
    chip, core = t // 2, lax.rem(t, 2)
    sibling = chip * 2 + 1 - core
    following = lax.rem(s + 1, sections)
    previous = lax.rem(s + sections - 1, sections)
    others = range(1, chips)

    def ahead(j):
        return lax.rem(chip + j, chips)

    def behind(j):
        return lax.rem(chip + chips - j, chips)

    def across(j):
        return {"tensor": ahead(j) * 2 + 1 - core}

    def deep(part):
        return slice(0, cut) if part == 0 else slice(cut, depth)

    def span(start, count):
        return pl.ds(pl.multiple_of(start * piece, piece), count * piece)

    def hidden_copy(j, part, m, d):
        lane = core if (part == 1) == (j == 0) else 1 - core
        first = pl.multiple_of((ahead(j) * 2 + lane) * local, local)
        return pltpu.make_async_copy(
            hidden.at[0, m, pl.ds(first, local), deep(d)], rows.at[j, part, m, :, deep(d)], hidden_sem.at[j, d]
        )

    def hidden_start(j, d):
        for part in range(2):
            for m in range(micro):
                hidden_copy(j, part, m, d).start()

    def all_of(ref, sem):
        return pltpu.make_async_copy(ref, ref, sem)

    def hidden_wait(j, d):
        all_of(rows.at[j, :, :, :, deep(d)], hidden_sem.at[j, d]).wait()

    def slab_copy(k, d):
        slot = lax.rem(k, SLABS)
        return pltpu.make_async_copy(
            weight.at[0, deep(d), span(2 * k, 2)], slab.at[slot, deep(d)], slab_sem.at[slot, d]
        )

    def first_copy(h, d):
        place = slice(h * piece, (h + 1) * piece)
        sem = first_sem.at[d] if h == 0 else slab_sem.at[0, d]
        return pltpu.make_async_copy(weight.at[0, deep(d), place], slab.at[0, deep(d), place], sem)

    def qkv_copy(p):
        place = span(4 * p, 4)
        return pltpu.make_async_copy(projector.at[0, place, :], qkv.at[place], qkv_sem)

    right_copy = pltpu.make_async_copy(projector.at[0, features - piece:, :], right_out, right_sem)

    res_copy = pltpu.make_async_copy(residual.at[0], res, res_sem)
    gain_copy = pltpu.make_async_copy(gain_in, gain, gain_sem)

    def carried_copy(u):
        return pltpu.make_async_copy(
            carried.at[core, chip, u], carried_out.at[0, :, :, span(u, 1)], carried_sem
        )

    def core_copy(k, j):
        place = pl.ds(2 * k, 2)
        return pltpu.make_async_remote_copy(
            src_ref=core_send.at[j, place], dst_ref=core_recv.at[j, place],
            send_sem=core_ss, recv_sem=core_rs.at[2 + lax.rem(k, 2), j - 1],
            device_id={"tensor": sibling}, device_id_type=MESH,
        )

    def core_half(h, j):
        return pltpu.make_async_remote_copy(
            src_ref=core_send.at[j, h], dst_ref=core_recv.at[j, h],
            send_sem=core_ss, recv_sem=core_rs.at[h, j - 1],
            device_id={"tensor": sibling}, device_id_type=MESH,
        )

    def mine_copy(p):
        place = pl.ds(4 * p, 4)
        return pltpu.make_async_remote_copy(
            src_ref=core_send.at[0, place], dst_ref=core_recv.at[0, place],
            send_sem=core_ss, recv_sem=mine_rs.at[p],
            device_id={"tensor": sibling}, device_id_type=MESH,
        )

    def x_part(k, j, place):
        return pltpu.make_async_remote_copy(
            src_ref=x_send.at[j - 1, place], dst_ref=x_recv.at[j - 1, place],
            send_sem=x_ss, recv_sem=x_rs.at[k, j - 1],
            device_id=across(j), device_id_type=MESH,
        )

    def x_copy(k, j):
        return x_part(k, j, pl.ds(2 * k, 2))

    def y_copy(p):
        place = pl.ds(4 * p, 4)
        return pltpu.make_async_remote_copy(
            src_ref=stream.at[place], dst_ref=carried.at[core, chip, place], send_sem=y_ss, recv_sem=y_rs.at[p],
            device_id={"section": following}, device_id_type=MESH,
        )

    def pair(p):
        return (p, 4 * p, 4)

    ends = [(final, 4 * final, 2), (final + 1, 4 * final + 2, 1), (final + 2, 4 * final + 3, 1)]

    def gather_copy(load, j, block):
        n, start, count = load
        place = carried.at[core, block, pl.ds(start, count)]
        return pltpu.make_async_remote_copy(
            src_ref=place, dst_ref=place, send_sem=g_ss.at[j - 1], recv_sem=g_rs.at[n, j - 1],
            device_id=across(j), device_id_type=MESH,
        )

    def gathered(load, j):
        n, start, count = load
        place = carried.at[1 - core, behind(j), pl.ds(start, count)]
        return pltpu.make_async_remote_copy(
            src_ref=place, dst_ref=place, send_sem=g_ss.at[j - 1], recv_sem=g_rs.at[n, j - 1],
            device_id=across(j), device_id_type=MESH,
        )

    def pass_out(load, j):
        n, start, count = load
        place = carried.at[core if j == 0 else 1 - core, behind(j), pl.ds(start, count)]
        return pltpu.make_async_remote_copy(
            src_ref=place, dst_ref=place, send_sem=c_ss.at[j], recv_sem=c_rs.at[n],
            device_id={"tensor": sibling}, device_id_type=MESH,
        )

    for d in range(2):
        for j in others:
            hidden_start(j, d)
        first_copy(0, d).start()

    barrier = pltpu.get_barrier_semaphore()
    pl.semaphore_signal(barrier, inc=1, device_id={"tensor": sibling}, device_id_type=MESH)
    for j in others:
        pl.semaphore_signal(barrier, inc=1, device_id=across(j), device_id_type=MESH)
    pl.semaphore_signal(barrier, inc=1, device_id={"section": following}, device_id_type=MESH)
    if sections > 2:
        pl.semaphore_signal(barrier, inc=1, device_id={"section": previous}, device_id_type=MESH)

    acc = (near_acc, far_acc)
    for ref in acc:
        ref[...] = jnp.zeros_like(ref)
    squares[...] = jnp.zeros_like(squares)

    def multiply(j, d, right):
        left = rows[j, :, :, :, d].reshape(2 * micro * local, -1)
        return jnp.dot(left, right, preferred_element_type=F32).reshape(2, micro, local, -1)

    def first_half(h, d):
        return slab[0, deep(d), h * piece:(h + 1) * piece]

    def first_product(h):
        for j in others:
            value = own[j - 1, h] + multiply(j, deep(1), first_half(h, 1))
            core_send[j, h] = value[0].astype(BF16)
            own[j - 1, h] = value

    for j in others:
        hidden_wait(j, 0)
    first_copy(0, 0).wait()
    for d in range(2):
        first_copy(1, d).start()
    for j in others:
        own[j - 1, 0] = multiply(j, deep(0), first_half(0, 0))
    for j in others:
        hidden_wait(j, 1)
    first_copy(0, 1).wait()
    for d in range(2):
        slab_copy(1, d).start()
    for d in range(2):
        hidden_start(0, d)
    first_product(0)
    pl.semaphore_wait(barrier, chips + (2 if sections > 2 else 1))
    for j in others:
        core_half(0, j).start()
    first_copy(1, 0).wait()
    for j in others:
        own[j - 1, 1] = multiply(j, deep(0), first_half(1, 0))
    first_copy(1, 1).wait()
    for k in range(2, SLABS):
        for d in range(2):
            slab_copy(k, d).start()
    first_product(1)
    for j in others:
        core_half(1, j).start()

    def first_send(h):
        for j in others:
            core_half(h, j).wait_recv()
            x_send[j - 1, h] = (own[j - 1, h, 1] + core_recv[j, h].astype(F32)).astype(BF16)
            x_part(0, j, h).start()

    first_send(0)
    res_copy.start()
    gain_copy.start()

    def side_lane(side, c):
        return lane_of(side, c, chip, core)

    def scaled(load, side):
        _, start, count = load
        values = []
        for n in range(count):
            blocks = [carried[side_lane(side, c), c, start + n].reshape(micro * local, piece) for c in range(chips)]
            values.append(jnp.concatenate(blocks, axis=0).astype(F32))
        values = values[0] if count == 1 else jnp.concatenate(values, axis=-1)
        squared = values * values
        part = squared[:, :128]
        for first in range(128, count * piece, 128):
            part = part + squared[:, first:first + 128]
        squares[side] += part
        return (values * gain[:, span(start, count)]).astype(BF16)

    def project(load, side):
        _, start, count = load
        acc[side][...] += jnp.dot(scaled(load, side), qkv[span(start, count)], preferred_element_type=F32)

    def scale(side):
        mean = jnp.sum(squares[side], axis=-1, keepdims=True) * (1.0 / features)
        return lax.rsqrt(mean + 1e-05)

    def hand(p, loads):
        y_copy(p).wait_recv()
        for load in loads:
            for j in others:
                gather_copy(load, j, chip).start()
        for load in loads:
            pass_out(load, 0).start()
        for n in range(4):
            carried_copy(4 * p + n).start()

    def relay(load):
        for j in others:
            gathered(load, j).wait_recv()
            pass_out(load, j).start()

    def relayed(load):
        n, start, count = load
        all_of(carried.at[core, :, pl.ds(start, count)], c_rs.at[n]).wait()

    def step(i, _):
        @pl.when(i < chunks)
        def _():
            slot = lax.rem(i, SLABS)
            for d in range(2):
                slab_copy(i, d).wait()
            for j in others:
                value = multiply(j, slice(None), slab[slot])
                for h in range(2):
                    core_send[j, 2 * i + h] = value[0, ..., h * piece:(h + 1) * piece].astype(BF16)
                core_copy(i, j).start()
                for h in range(2):
                    held[j - 1, h] = value[1, ..., h * piece:(h + 1) * piece]

        @pl.when(i == 1)
        def _():
            first_send(1)
            for d in range(2):
                hidden_wait(0, d)

        @pl.when(i <= chunks)
        def _():
            k = i - 1
            value = multiply(0, slice(None), slab[lax.rem(k, SLABS)])
            for h in range(2):
                core_send[0, 2 * k + h] = value[0, ..., h * piece:(h + 1) * piece].astype(BF16)
                base[2 * k + h] = value[1, ..., h * piece:(h + 1) * piece]

            @pl.when(lax.rem(k, 2) == 1)
            def _():
                mine_copy(k // 2).start()

            @pl.when(k + SLABS < chunks)
            def _():
                for d in range(2):
                    slab_copy(k + SLABS, d).start()

        @pl.when(i < chunks)
        def _():
            for j in others:
                core_copy(i, j).wait_recv()
                for h in range(2):
                    x_send[j - 1, 2 * i + h] = (held[j - 1, h] + core_recv[j, 2 * i + h].astype(F32)).astype(BF16)
                x_copy(i, j).start()

        k_sum = i - LAG_SUM

        @pl.when((k_sum >= 0) & (k_sum < chunks))
        def _():
            k = k_sum
            p = k // 2

            @pl.when(k == 0)
            def _():
                res_copy.wait()
                gain_copy.wait()
                right_copy.start()

            @pl.when(lax.rem(k, 2) == 0)
            def _():
                qkv_copy(p).start()
                mine_copy(p).wait_recv()

            for j in others:
                x_copy(k, j).wait_recv()
            for h in range(2):
                u = 2 * k + h
                value = base[u] + core_recv[0, u].astype(F32)
                for j in others:
                    value = value + x_recv[j - 1, u].astype(F32)
                stream[u] = (value + res[:, :, span(u, 1)].astype(F32)).astype(BF16)

            @pl.when(lax.rem(k, 2) == 1)
            def _():
                y_copy(p).start()

        k_hand = i - LAG_HAND

        @pl.when((k_hand >= 0) & (lax.rem(k_hand, 2) == 0))
        def _():
            hand(k_hand // 2, [pair(k_hand // 2)])

        return 0

    stop = chunks + LAG_SUM
    lax.fori_loop(1, stop, step, 0)
    begun = (stop - 1 - LAG_HAND) // 2 + 1
    for p in range(begun, final):
        hand(p, [pair(p)])

    def work(p, _):
        relay(pair(p))

        @pl.when(p == 0)
        def _():
            all_of(qkv, qkv_sem).wait()

        project(pair(p), 0)

        @pl.when(p == 0)
        def _():
            hand(final, ends)

        relayed(pair(p))
        project(pair(p), 1)
        return 0

    lax.fori_loop(0, final, work, 0)

    for load in ends[:-1]:
        relay(load)
        project(load, 0)
    relayed(ends[0])
    project(ends[0], 1)
    right_copy.wait()
    relay(ends[-1])
    relayed(ends[1])
    project(ends[1], 1)
    project(ends[-1], 0)
    near_out[...] = (near_acc[...] * scale(0)).astype(BF16)
    relayed(ends[-1])
    far_last[...] = scaled(ends[-1], 1)
    far_scale[...] = jnp.broadcast_to(scale(1), far_scale.shape)

    all_of(core_send, core_ss).wait()
    all_of(x_send, x_ss).wait()
    all_of(stream, y_ss).wait()
    all_of(carried_out.at[0], carried_sem).wait()
    all_of(carried.at[core, chip], c_ss.at[0]).wait()
    for j in others:
        all_of(carried.at[core, chip], g_ss.at[j - 1]).wait()
        all_of(carried.at[1 - core, behind(j)], c_ss.at[j]).wait()


def leave(
    tensor, carried_in, near_in, far_acc, far_last, far_scale, right, carried_out, projected_out,
    far, carried_sem, near_sem, far_sem,
):
    chips = tensor // 2
    micro, local = carried_in.shape[1:3]
    t = lax.axis_index("tensor")
    chip, core = t // 2, lax.rem(t, 2)
    carried_copy = pltpu.make_async_copy(carried_in, carried_out, carried_sem)

    def out_copies(ref, side, sem):
        copies = []
        for c in range(chips):
            first = pl.multiple_of((c * 2 + lane_of(side, c, chip, core)) * local, local)
            for m in range(micro):
                lines = pl.ds((c * micro + m) * local, local)
                copies.append(pltpu.make_async_copy(
                    ref.at[lines], projected_out.at[0, m, pl.ds(first, local), :], sem
                ))
        return copies

    near_copies = out_copies(near_in, 0, near_sem)
    far_copies = out_copies(far, 1, far_sem)
    carried_copy.start()
    for copy in near_copies:
        copy.start()
    value = far_acc[...] + jnp.dot(far_last[...], right[...], preferred_element_type=F32)
    far[...] = (value * far_scale[:, :1]).astype(BF16)
    for copy in far_copies:
        copy.start()
    carried_copy.wait()
    for ref, sem in ((near_in, near_sem), (far, far_sem)):
        pltpu.make_async_copy(ref, ref, sem).wait()


def per_device(sections, tensor, hidden, down_weight, residual, norm_gain, qkv_weight):
    _, micro, tokens, depth = hidden.shape
    local, features = residual.shape[2:]
    outputs = qkv_weight.shape[2]
    chips = tensor // 2
    chunks = CHUNKS
    width = features // chunks
    piece = width // 2
    units, pairs = 2 * chunks, chunks // 2
    dma = pltpu.SemaphoreType.DMA
    anywhere = pl.BlockSpec(memory_space=pl.ANY)
    carried_shape = (1, micro, local, features)
    projected_shape = (1, micro, tokens, outputs)
    lines = micro * tokens // 2
    results = pl.pallas_call(
        functools.partial(kernel, sections, tensor),
        out_shape=(
            pltpu.VMEM(carried_shape, BF16),
            pltpu.VMEM((lines, outputs), BF16),
            pltpu.VMEM((lines, outputs), F32),
            pltpu.VMEM((lines, piece), BF16),
            pltpu.VMEM((lines, 128), F32),
            pltpu.VMEM((piece, outputs), BF16),
        ),
        in_specs=[pl.BlockSpec(memory_space=pltpu.HBM)] * 5,
        out_specs=(pl.BlockSpec(memory_space=pltpu.VMEM),) * 6,
        scratch_shapes=[
            pltpu.VMEM((chips, 2, micro, local, depth), BF16),
            pltpu.VMEM((SLABS, depth, width), BF16),
            pltpu.VMEM((features, outputs), BF16),
            pltpu.VMEM((micro, local, features), BF16),
            pltpu.VMEM((1, features), F32),
            pltpu.VMEM((chips - 1, 2, 2, micro, local, piece), F32),
            pltpu.VMEM((chips - 1, 2, micro, local, piece), F32),
            pltpu.VMEM((chips, units, micro, local, piece), BF16),
            pltpu.VMEM((chips, units, micro, local, piece), BF16),
            pltpu.VMEM((chips - 1, units, micro, local, piece), BF16),
            pltpu.VMEM((chips - 1, units, micro, local, piece), BF16),
            pltpu.VMEM((units, micro, local, piece), F32),
            pltpu.VMEM((units, micro, local, piece), BF16),
            pltpu.VMEM((2, chips, units, micro, local, piece), BF16),
            pltpu.VMEM((lines, outputs), F32),
            pltpu.VMEM((2, lines, 128), F32),
            dma((chips, 2)), dma((SLABS, 2)), dma((2,)), dma, dma, dma, dma, dma,
            dma, dma((4, chips - 1)), dma((pairs,)), dma, dma((chunks, chips - 1)), dma, dma((pairs,)),
            dma((chips - 1,)), dma((pairs + 2, chips - 1)), dma((chips,)), dma((pairs + 2,)),
        ],
        compiler_params=pltpu.CompilerParams(
            collective_id=0, has_side_effects=True, vmem_limit_bytes=50 * 1024 * 1024
        ),
    )(
        hidden,
        down_weight,
        pltpu.with_memory_space_constraint(residual, pltpu.HBM),
        pltpu.with_memory_space_constraint(norm_gain, pltpu.HBM),
        qkv_weight,
    )
    return pl.pallas_call(
        functools.partial(leave, tensor),
        out_shape=(
            jax.ShapeDtypeStruct(carried_shape, BF16),
            jax.ShapeDtypeStruct(projected_shape, BF16),
        ),
        in_specs=[pl.BlockSpec(memory_space=pltpu.VMEM)] * 6,
        out_specs=(anywhere,) * 2,
        scratch_shapes=[pltpu.VMEM((lines, outputs), BF16), dma, dma, dma],
        compiler_params=pltpu.CompilerParams(vmem_limit_bytes=8 * 1024 * 1024),
    )(*(pltpu.with_memory_space_constraint(x, pltpu.VMEM) for x in results))


def solution(mesh):
    placed = (
        P("section", "dp", None, "tensor"),
        P("section", "tensor", None),
        P("section", "dp", "tensor", None),
        P("section", None),
        P("section", None, "tensor"),
    )
    return jax.shard_map(
        functools.partial(per_device, mesh.shape["section"], mesh.shape["tensor"]),
        mesh=mesh,
        in_specs=placed,
        out_specs=(P("section", "dp", "tensor", None), P("section", "dp", None, "tensor")),
        check_vma=False,
    )
```

```python
import functools

import jax
import jax.numpy as jnp
from jax import lax
from jax.experimental import pallas as pl
from jax.experimental.pallas import tpu as pltpu
from jax.sharding import PartitionSpec as P

MESH = pl.DeviceIdType.MESH
F32 = jnp.float32
BF16 = jnp.bfloat16
CHUNKS = 8
SLABS = 3
LAG_SUM, LAG_HAND = 3, 9


def lane_of(side, c, chip, core):
    return jnp.where(c == chip, core, 1 - core) if side == 0 else jnp.where(c == chip, 1 - core, core)


def kernel(
    sections, tensor, hidden, weight, residual, gain_in, projector,
    carried_out, near_out, far_acc, far_last, far_mean, right_out,
    rows, slab, qkv, res, gain, own, held, core_send, core_recv, x_send, x_recv, base, stream, carried, near_acc, squares,
    hidden_sem, slab_sem, first_sem, qkv_sem, right_sem, res_sem, gain_sem, carried_sem,
    core_ss, core_rs, mine_rs, x_ss, x_rs, y_ss, y_rs, g_ss, g_rs, c_ss, c_rs,
):
    chips = tensor // 2
    units, micro, local, piece = stream.shape
    chunks = units // 2
    width = 2 * piece
    features = units * piece
    depth = rows.shape[-1]
    cut = pl.cdiv(depth // 2, 128) * 128
    lines = chips * micro * local
    pairs = chunks // 2
    final = pairs - 1
    s = lax.axis_index("section")
    t = lax.axis_index("tensor")
    chip, core = t // 2, lax.rem(t, 2)
    sibling = chip * 2 + 1 - core
    following = lax.rem(s + 1, sections)
    previous = lax.rem(s + sections - 1, sections)
    others = range(1, chips)

    def ahead(j):
        return lax.rem(chip + j, chips)

    def behind(j):
        return lax.rem(chip + chips - j, chips)

    def across(j):
        return {"tensor": ahead(j) * 2 + 1 - core}

    def deep(part):
        return slice(0, cut) if part == 0 else slice(cut, depth)

    def span(start, count):
        return pl.ds(pl.multiple_of(start * piece, piece), count * piece)

    def hidden_copy(j, part, m, d):
        lane = core if (part == 1) == (j == 0) else 1 - core
        first = pl.multiple_of((ahead(j) * 2 + lane) * local, local)
        return pltpu.make_async_copy(
            hidden.at[0, m, pl.ds(first, local), deep(d)], rows.at[j, part, m, :, deep(d)], hidden_sem.at[j, d]
        )

    def hidden_start(j, d):
        for part in range(2):
            for m in range(micro):
                hidden_copy(j, part, m, d).start()

    def all_of(ref, sem):
        return pltpu.make_async_copy(ref, ref, sem)

    def hidden_wait(j, d):
        all_of(rows.at[j, :, :, :, deep(d)], hidden_sem.at[j, d]).wait()

    def slab_copy(k, d):
        slot = lax.rem(k, SLABS)
        return pltpu.make_async_copy(
            weight.at[0, deep(d), span(2 * k, 2)], slab.at[slot, deep(d)], slab_sem.at[slot, d]
        )

    def first_copy(h, d):
        place = slice(h * piece, (h + 1) * piece)
        sem = first_sem.at[d] if h == 0 else slab_sem.at[0, d]
        return pltpu.make_async_copy(weight.at[0, deep(d), place], slab.at[0, deep(d), place], sem)

    def qkv_copy(p):
        place = span(4 * p, 4)
        return pltpu.make_async_copy(projector.at[0, place, :], qkv.at[place], qkv_sem)

    right_copy = pltpu.make_async_copy(projector.at[0, features - piece:, :], right_out, right_sem)

    res_copy = pltpu.make_async_copy(residual.at[0], res, res_sem)
    gain_copy = pltpu.make_async_copy(gain_in, gain, gain_sem)

    def carried_copy(u):
        return pltpu.make_async_copy(
            carried.at[core, chip, u], carried_out.at[0, :, :, span(u, 1)], carried_sem
        )

    def core_copy(k, j):
        place = pl.ds(2 * k, 2)
        return pltpu.make_async_remote_copy(
            src_ref=core_send.at[j, place], dst_ref=core_recv.at[j, place],
            send_sem=core_ss, recv_sem=core_rs.at[2 + lax.rem(k, 2), j - 1],
            device_id={"tensor": sibling}, device_id_type=MESH,
        )

    def core_half(h, j):
        return pltpu.make_async_remote_copy(
            src_ref=core_send.at[j, h], dst_ref=core_recv.at[j, h],
            send_sem=core_ss, recv_sem=core_rs.at[h, j - 1],
            device_id={"tensor": sibling}, device_id_type=MESH,
        )

    def mine_copy(p):
        place = pl.ds(4 * p, 4)
        return pltpu.make_async_remote_copy(
            src_ref=core_send.at[0, place], dst_ref=core_recv.at[0, place],
            send_sem=core_ss, recv_sem=mine_rs.at[p],
            device_id={"tensor": sibling}, device_id_type=MESH,
        )

    def x_part(k, j, place):
        return pltpu.make_async_remote_copy(
            src_ref=x_send.at[j - 1, place], dst_ref=x_recv.at[j - 1, place],
            send_sem=x_ss, recv_sem=x_rs.at[k, j - 1],
            device_id=across(j), device_id_type=MESH,
        )

    def x_copy(k, j):
        return x_part(k, j, pl.ds(2 * k, 2))

    def y_copy(p):
        place = pl.ds(4 * p, 4)
        return pltpu.make_async_remote_copy(
            src_ref=stream.at[place], dst_ref=carried.at[core, chip, place], send_sem=y_ss, recv_sem=y_rs.at[p],
            device_id={"section": following}, device_id_type=MESH,
        )

    def pair(p):
        return (p, 4 * p, 4)

    ends = [(final, 4 * final, 2), (final + 1, 4 * final + 2, 1), (final + 2, 4 * final + 3, 1)]

    def gather_copy(load, j, block):
        n, start, count = load
        place = carried.at[core, block, pl.ds(start, count)]
        return pltpu.make_async_remote_copy(
            src_ref=place, dst_ref=place, send_sem=g_ss.at[j - 1], recv_sem=g_rs.at[n, j - 1],
            device_id=across(j), device_id_type=MESH,
        )

    def gathered(load, j):
        n, start, count = load
        place = carried.at[1 - core, behind(j), pl.ds(start, count)]
        return pltpu.make_async_remote_copy(
            src_ref=place, dst_ref=place, send_sem=g_ss.at[j - 1], recv_sem=g_rs.at[n, j - 1],
            device_id=across(j), device_id_type=MESH,
        )

    def pass_out(load, j):
        n, start, count = load
        place = carried.at[core if j == 0 else 1 - core, behind(j), pl.ds(start, count)]
        return pltpu.make_async_remote_copy(
            src_ref=place, dst_ref=place, send_sem=c_ss.at[j], recv_sem=c_rs.at[n],
            device_id={"tensor": sibling}, device_id_type=MESH,
        )

    for d in range(2):
        for j in others:
            hidden_start(j, d)
        first_copy(0, d).start()

    barrier = pltpu.get_barrier_semaphore()
    pl.semaphore_signal(barrier, inc=1, device_id={"tensor": sibling}, device_id_type=MESH)
    for j in others:
        pl.semaphore_signal(barrier, inc=1, device_id=across(j), device_id_type=MESH)
    pl.semaphore_signal(barrier, inc=1, device_id={"section": following}, device_id_type=MESH)
    if sections > 2:
        pl.semaphore_signal(barrier, inc=1, device_id={"section": previous}, device_id_type=MESH)

    acc = (near_acc, far_acc)
    for ref in acc:
        ref[...] = jnp.zeros_like(ref)
    squares[...] = jnp.zeros_like(squares)

    def multiply(j, d, right):
        left = rows[j, :, :, :, d].reshape(2 * micro * local, -1)
        return jnp.dot(left, right, preferred_element_type=F32).reshape(2, micro, local, -1)

    def first_half(h, d):
        return slab[0, deep(d), h * piece:(h + 1) * piece]

    def first_product(h):
        for j in others:
            value = own[j - 1, h] + multiply(j, deep(1), first_half(h, 1))
            core_send[j, h] = value[0].astype(BF16)
            own[j - 1, h] = value

    for j in others:
        hidden_wait(j, 0)
    first_copy(0, 0).wait()
    for d in range(2):
        first_copy(1, d).start()
    for j in others:
        own[j - 1, 0] = multiply(j, deep(0), first_half(0, 0))
    for j in others:
        hidden_wait(j, 1)
    first_copy(0, 1).wait()
    for d in range(2):
        slab_copy(1, d).start()
    for d in range(2):
        hidden_start(0, d)
    first_product(0)
    pl.semaphore_wait(barrier, chips + (2 if sections > 2 else 1))
    for j in others:
        core_half(0, j).start()
    first_copy(1, 0).wait()
    for j in others:
        own[j - 1, 1] = multiply(j, deep(0), first_half(1, 0))
    first_copy(1, 1).wait()
    for k in range(2, SLABS):
        for d in range(2):
            slab_copy(k, d).start()
    first_product(1)
    for j in others:
        core_half(1, j).start()

    def first_send(h):
        for j in others:
            core_half(h, j).wait_recv()
            x_send[j - 1, h] = (own[j - 1, h, 1] + core_recv[j, h].astype(F32)).astype(BF16)
            x_part(0, j, h).start()

    first_send(0)
    res_copy.start()
    gain_copy.start()

    def side_lane(side, c):
        return lane_of(side, c, chip, core)

    def scaled(load, side):
        _, start, count = load
        values = []
        for n in range(count):
            blocks = [carried[side_lane(side, c), c, start + n].reshape(micro * local, piece) for c in range(chips)]
            values.append(jnp.concatenate(blocks, axis=0).astype(F32))
        values = values[0] if count == 1 else jnp.concatenate(values, axis=-1)
        squared = values * values
        part = squared[:, :128]
        for first in range(128, count * piece, 128):
            part = part + squared[:, first:first + 128]
        squares[side] += part
        return (values * gain[:, span(start, count)]).astype(BF16)

    def project(load, side):
        _, start, count = load
        acc[side][...] += jnp.dot(scaled(load, side), qkv[span(start, count)], preferred_element_type=F32)

    def scale(side):
        mean = jnp.sum(squares[side], axis=-1, keepdims=True) * (1.0 / features)
        return lax.rsqrt(mean + 1e-05)

    def hand(p, loads):
        y_copy(p).wait_recv()
        for load in loads:
            for j in others:
                gather_copy(load, j, chip).start()
        for load in loads:
            pass_out(load, 0).start()
        for n in range(4):
            carried_copy(4 * p + n).start()

    def relay(load):
        for j in others:
            gathered(load, j).wait_recv()
            pass_out(load, j).start()

    def relayed(load):
        n, start, count = load
        all_of(carried.at[core, :, pl.ds(start, count)], c_rs.at[n]).wait()

    def step(i, _):
        @pl.when(i < chunks)
        def _():
            slot = lax.rem(i, SLABS)
            for d in range(2):
                slab_copy(i, d).wait()
            for j in others:
                value = multiply(j, slice(None), slab[slot])
                for h in range(2):
                    core_send[j, 2 * i + h] = value[0, ..., h * piece:(h + 1) * piece].astype(BF16)
                core_copy(i, j).start()
                for h in range(2):
                    held[j - 1, h] = value[1, ..., h * piece:(h + 1) * piece]

        @pl.when(i == 1)
        def _():
            first_send(1)
            for d in range(2):
                hidden_wait(0, d)

        @pl.when(i <= chunks)
        def _():
            k = i - 1
            value = multiply(0, slice(None), slab[lax.rem(k, SLABS)])
            for h in range(2):
                core_send[0, 2 * k + h] = value[0, ..., h * piece:(h + 1) * piece].astype(BF16)
                base[2 * k + h] = value[1, ..., h * piece:(h + 1) * piece]

            @pl.when(lax.rem(k, 2) == 1)
            def _():
                mine_copy(k // 2).start()

            @pl.when(k + SLABS < chunks)
            def _():
                for d in range(2):
                    slab_copy(k + SLABS, d).start()

        @pl.when(i < chunks)
        def _():
            for j in others:
                core_copy(i, j).wait_recv()
                for h in range(2):
                    x_send[j - 1, 2 * i + h] = (held[j - 1, h] + core_recv[j, 2 * i + h].astype(F32)).astype(BF16)
                x_copy(i, j).start()

        k_sum = i - LAG_SUM

        @pl.when((k_sum >= 0) & (k_sum < chunks))
        def _():
            k = k_sum
            p = k // 2

            @pl.when(k == 0)
            def _():
                res_copy.wait()
                gain_copy.wait()
                right_copy.start()

            @pl.when(lax.rem(k, 2) == 0)
            def _():
                qkv_copy(p).start()
                mine_copy(p).wait_recv()

            for j in others:
                x_copy(k, j).wait_recv()
            for h in range(2):
                u = 2 * k + h
                value = base[u] + core_recv[0, u].astype(F32)
                for j in others:
                    value = value + x_recv[j - 1, u].astype(F32)
                stream[u] = (value + res[:, :, span(u, 1)].astype(F32)).astype(BF16)

            @pl.when(lax.rem(k, 2) == 1)
            def _():
                y_copy(p).start()

        k_hand = i - LAG_HAND

        @pl.when((k_hand >= 0) & (lax.rem(k_hand, 2) == 0))
        def _():
            hand(k_hand // 2, [pair(k_hand // 2)])

        return 0

    stop = chunks + LAG_SUM
    lax.fori_loop(1, stop, step, 0)
    begun = (stop - 1 - LAG_HAND) // 2 + 1
    for p in range(begun, final):
        hand(p, [pair(p)])

    def work(p, _):
        relay(pair(p))

        @pl.when(p == 0)
        def _():
            all_of(qkv, qkv_sem).wait()

        project(pair(p), 0)

        @pl.when(p == 0)
        def _():
            hand(final, ends)

        relayed(pair(p))
        project(pair(p), 1)
        return 0

    lax.fori_loop(0, final, work, 0)

    for load in ends[:-1]:
        relay(load)
        project(load, 0)
    relayed(ends[0])
    project(ends[0], 1)
    right_copy.wait()
    relay(ends[-1])
    relayed(ends[1])
    project(ends[1], 1)
    project(ends[-1], 0)
    near_out[...] = (near_acc[...] * scale(0)).astype(BF16)
    relayed(ends[-1])
    far_last[...] = scaled(ends[-1], 1)
    far_mean[...] = squares[1] * (1.0 / features)

    all_of(core_send, core_ss).wait()
    all_of(x_send, x_ss).wait()
    all_of(stream, y_ss).wait()
    all_of(carried_out.at[0], carried_sem).wait()
    all_of(carried.at[core, chip], c_ss.at[0]).wait()
    for j in others:
        all_of(carried.at[core, chip], g_ss.at[j - 1]).wait()
        all_of(carried.at[1 - core, behind(j)], c_ss.at[j]).wait()


def leave(
    tensor, carried_in, near_in, far_acc, far_last, far_mean, right, carried_out, projected_out,
    far, carried_sem, near_sem, far_sem,
):
    chips = tensor // 2
    micro, local = carried_in.shape[1:3]
    t = lax.axis_index("tensor")
    chip, core = t // 2, lax.rem(t, 2)
    carried_copy = pltpu.make_async_copy(carried_in, carried_out, carried_sem)

    def out_copies(ref, side, sem):
        copies = []
        for c in range(chips):
            first = pl.multiple_of((c * 2 + lane_of(side, c, chip, core)) * local, local)
            for m in range(micro):
                lines = pl.ds((c * micro + m) * local, local)
                copies.append(pltpu.make_async_copy(
                    ref.at[lines], projected_out.at[0, m, pl.ds(first, local), :], sem
                ))
        return copies

    near_copies = out_copies(near_in, 0, near_sem)
    far_copies = out_copies(far, 1, far_sem)
    carried_copy.start()
    for copy in near_copies:
        copy.start()
    value = far_acc[...] + jnp.dot(far_last[...], right[...], preferred_element_type=F32)
    mean = jnp.sum(far_mean[...], axis=-1, keepdims=True)
    far[...] = (value * lax.rsqrt(mean + 1e-05)).astype(BF16)
    for copy in far_copies:
        copy.start()
    carried_copy.wait()
    for ref, sem in ((near_in, near_sem), (far, far_sem)):
        pltpu.make_async_copy(ref, ref, sem).wait()


def per_device(sections, tensor, hidden, down_weight, residual, norm_gain, qkv_weight):
    _, micro, tokens, depth = hidden.shape
    local, features = residual.shape[2:]
    outputs = qkv_weight.shape[2]
    chips = tensor // 2
    chunks = CHUNKS
    width = features // chunks
    piece = width // 2
    units, pairs = 2 * chunks, chunks // 2
    dma = pltpu.SemaphoreType.DMA
    anywhere = pl.BlockSpec(memory_space=pl.ANY)
    carried_shape = (1, micro, local, features)
    projected_shape = (1, micro, tokens, outputs)
    lines = micro * tokens // 2
    results = pl.pallas_call(
        functools.partial(kernel, sections, tensor),
        out_shape=(
            pltpu.VMEM(carried_shape, BF16),
            pltpu.VMEM((lines, outputs), BF16),
            pltpu.VMEM((lines, outputs), F32),
            pltpu.VMEM((lines, piece), BF16),
            pltpu.VMEM((lines, 128), F32),
            pltpu.VMEM((piece, outputs), BF16),
        ),
        in_specs=[pl.BlockSpec(memory_space=pltpu.HBM)] * 5,
        out_specs=(pl.BlockSpec(memory_space=pltpu.VMEM),) * 6,
        scratch_shapes=[
            pltpu.VMEM((chips, 2, micro, local, depth), BF16),
            pltpu.VMEM((SLABS, depth, width), BF16),
            pltpu.VMEM((features, outputs), BF16),
            pltpu.VMEM((micro, local, features), BF16),
            pltpu.VMEM((1, features), F32),
            pltpu.VMEM((chips - 1, 2, 2, micro, local, piece), F32),
            pltpu.VMEM((chips - 1, 2, micro, local, piece), F32),
            pltpu.VMEM((chips, units, micro, local, piece), BF16),
            pltpu.VMEM((chips, units, micro, local, piece), BF16),
            pltpu.VMEM((chips - 1, units, micro, local, piece), BF16),
            pltpu.VMEM((chips - 1, units, micro, local, piece), BF16),
            pltpu.VMEM((units, micro, local, piece), F32),
            pltpu.VMEM((units, micro, local, piece), BF16),
            pltpu.VMEM((2, chips, units, micro, local, piece), BF16),
            pltpu.VMEM((lines, outputs), F32),
            pltpu.VMEM((2, lines, 128), F32),
            dma((chips, 2)), dma((SLABS, 2)), dma((2,)), dma, dma, dma, dma, dma,
            dma, dma((4, chips - 1)), dma((pairs,)), dma, dma((chunks, chips - 1)), dma, dma((pairs,)),
            dma((chips - 1,)), dma((pairs + 2, chips - 1)), dma((chips,)), dma((pairs + 2,)),
        ],
        compiler_params=pltpu.CompilerParams(
            collective_id=0, has_side_effects=True, vmem_limit_bytes=50 * 1024 * 1024
        ),
    )(
        hidden,
        down_weight,
        pltpu.with_memory_space_constraint(residual, pltpu.HBM),
        pltpu.with_memory_space_constraint(norm_gain, pltpu.HBM),
        qkv_weight,
    )
    return pl.pallas_call(
        functools.partial(leave, tensor),
        out_shape=(
            jax.ShapeDtypeStruct(carried_shape, BF16),
            jax.ShapeDtypeStruct(projected_shape, BF16),
        ),
        in_specs=[pl.BlockSpec(memory_space=pltpu.VMEM)] * 6,
        out_specs=(anywhere,) * 2,
        scratch_shapes=[pltpu.VMEM((lines, outputs), BF16), dma, dma, dma],
        compiler_params=pltpu.CompilerParams(vmem_limit_bytes=8 * 1024 * 1024),
    )(*(pltpu.with_memory_space_constraint(x, pltpu.VMEM) for x in results))


def solution(mesh):
    placed = (
        P("section", "dp", None, "tensor"),
        P("section", "tensor", None),
        P("section", "dp", "tensor", None),
        P("section", None),
        P("section", None, "tensor"),
    )
    return jax.shard_map(
        functools.partial(per_device, mesh.shape["section"], mesh.shape["tensor"]),
        mesh=mesh,
        in_specs=placed,
        out_specs=(P("section", "dp", "tensor", None), P("section", "dp", None, "tensor")),
        check_vma=False,
    )
```
